32 devices in a mesh: groups: 2 (over x), role: 2 (over core), seq: 8 (over z, y).
Axes of the slice: x: 2, y: 2, z: 4, core: 2. Of those that a mesh axis runs over, the one named last changes fastest.
Arguments:
- kv_store: bfloat16 [2, 8192, 1024], P('role', ('groups', 'seq')), parts along dimension 1, may hold values from -6 to 6
- queries: bfloat16 [2, 256, 2, 4096], P('role', ('groups', 'seq')), parts along dimension 1, may hold values from -100 to 100
- step_kv: bfloat16 [256, 2, 1024], P(('groups', 'seq')), parts along dimension 0, may hold values from -6 to 6
- suffix_pages: int32 [256, 2], P(('groups', 'seq')), parts along dimension 0, may hold values from 0 to 31, as said below
- suffix_len: int32 [256], P(('groups', 'seq')), parts along dimension 0, may hold values from 2 to 32, as said below
- owner: int32 [256, 1], P(('groups', 'seq')), parts along dimension 0, may hold values from 0 to 7; in each aligned block of 16 rows (0 to 15, 16 to 31, ...) at most 4 rows name the same one
- parent_id: int32 [256], P(('groups', 'seq')), parts along dimension 0, may hold values from 0 to 1
- parent_pages: int32 [32, 16], P(('groups', 'seq')), parts along dimension 0, may hold values from 0 to 31, as said below
- parent_len: int32 [32], P(('groups', 'seq')), parts along dimension 0, may hold values from 1 to 256, as said below
Outputs:
- served: bfloat16 [2, 256, 2, 4096], P('role', ('groups', 'seq')), parts along dimension 1
The draws below stay inside these ranges and needn't reach their ends.
There are 2 independent parts, one for each index of `groups`. The reference program is written for one: setup_inputs(seed, part) draws one part's arguments, and reference() takes and returns one part's arrays. A program takes and returns all parts, laid end to end along the dimension named above; each array names one. Nothing has to cross between parts.
Inputs may be any that keep to these rules, and one draw needn't show every extreme that they name: `suffix_pages`: on each device the page lists of its 16 requests are disjoint and together name every page of its store once. `suffix_len`: the first request of every device has the full 32 tokens. Of the requests of one device at most 4 go to one owner, and some device sends 4 to one owner. `parent_pages`: on each device the page tables of its 2 parent slots are disjoint and together name every page of its store once. `parent_len`: the first parent slot of every device has the full 256 tokens.
All inputs are finite; a program needn't handle non-finite values.
Results may differ from the reference program's by a relative error of at most 0.0025.
Values may be sent and summed in bfloat16 or wider, within the bound.
A program may use at most 128 MiB of HBM per device.

```python
import math
import jax
import jax.numpy as jnp
import numpy as np
from jax import lax

HEAD_DIM = 128
KV_HEADS = 4
GROUP = 8
PAGE = 16
SUF_PAGES = 2
REQ_DEV = 16
PARENTS = 2
QW = 4096
KVW = 1024
SUF = 32
STORE_PAGES = 32
PAR_PAGES = 16
PCTX = 256
CAP = 4
REQUESTS = 128
PAR_ALL = 16
N_SEQ = 8


def shared_draws(key):
    key_store = jax.random.fold_in(key, 101)
    key_query = jax.random.fold_in(key, 102)
    key_step = jax.random.fold_in(key, 103)
    key_pages = jax.random.fold_in(key, 104)
    devices = REQUESTS // REQ_DEV
    page_store = jnp.clip(jax.random.normal(key_store, (2, devices * STORE_PAGES * PAGE, KVW), jnp.float32), -6.0, 6.0)
    query_rows = jnp.clip(2.5 * jax.random.normal(key_query, (2, REQUESTS, 2, QW), jnp.float32), -15.0, 15.0)
    step_rows = jnp.clip(jax.random.normal(key_step, (REQUESTS, 2, KVW), jnp.float32), -6.0, 6.0)
    page_keys = jax.random.split(key_pages, devices)
    page_lists = jax.vmap(lambda subkey: jax.random.permutation(subkey, STORE_PAGES))(page_keys)
    page_lists = page_lists.reshape(REQUESTS, SUF_PAGES).astype(jnp.int32)
    return (page_store, query_rows, step_rows, page_lists)


def draw_kv_store(key, part):
    return shared_draws(key)[0].astype(jnp.bfloat16)


def draw_queries(key, part):
    return shared_draws(key)[1].astype(jnp.bfloat16)


def draw_step_kv(key, part):
    return shared_draws(key)[2].astype(jnp.bfloat16)


def draw_suffix_pages(key, part):
    return shared_draws(key)[3]


def draw_suffix_len(key, part):
    lengths = jax.random.randint(jax.random.fold_in(key, 201), (REQUESTS,), 2, SUF + 1, jnp.int32)
    return lengths.at[::REQ_DEV].set(SUF)


def draw_parent_pages(key, part):
    devices = REQUESTS // REQ_DEV
    page_keys = jax.random.split(jax.random.fold_in(key, 202), devices)
    page_lists = jax.vmap(lambda subkey: jax.random.permutation(subkey, STORE_PAGES))(page_keys)
    return page_lists.reshape(devices * PARENTS, PAR_PAGES).astype(jnp.int32)


def draw_parent_len(key, part):
    lengths = jax.random.randint(jax.random.fold_in(key, 203), (PAR_ALL,), 1, PCTX + 1, jnp.int32)
    return lengths.at[::PARENTS].set(PCTX)


def plant(values, stream_key, least, top_value):
    place = [jax.random.randint(jax.random.fold_in(stream_key, axis), (), 0, length) for axis, length in enumerate(values.shape)]
    longest = values.shape.index(max(values.shape))
    beside = place[:longest] + [(place[longest] + 1) % values.shape[longest]] + place[longest + 1:]
    return values.at[tuple(place)].set(least).at[tuple(beside)].set(top_value)


def routed_block(key, own, number, rows, number_of, top, reach, slope):
    sequence = jax.random.permutation(key, number_of)
    heavy_load, common = portions_of(number_of, rows * top, reach, slope, True), portions_of(number_of, rows * top, reach, slope, False)
    places = jnp.arange(number_of)

    def named(tallies, offset_by):
        used = int((tallies > 0).sum())
        fixed = max(1, used // 4)
        moved = fixed + (places - fixed + offset_by * (used - fixed)) % max(1, number_of - fixed)
        return jnp.zeros((number_of,), jnp.int32).at[sequence[jnp.where(places < fixed, places, moved)]].set(jnp.asarray(tallies, jnp.int32))

    tallies = jnp.where(number % 4 == 0, named(heavy_load, number // 4), named(common, number - number // 4 - 1))
    mixed = jax.random.permutation(jax.random.fold_in(own, 3), number_of)
    source_of, taker = mixed[0:number_of // 2 * 2:2], mixed[1:number_of // 2 * 2:2]
    room = jnp.minimum(tallies[source_of] - 1, reach - tallies[taker]) // 2
    room = jnp.where((source_of == sequence[0]) | (taker == sequence[0]) | (tallies[taker] == 0), 0, jnp.maximum(room, 0))
    moved = jax.random.randint(jax.random.fold_in(own, 4), (number_of // 2,), 0, 1 << 20) % (room + 1)
    tallies = tallies.at[source_of].add(-moved).at[taker].add(moved)
    members = jnp.searchsorted(jnp.cumsum(tallies), jnp.arange(rows * top), side="right").astype(jnp.int32)
    table = members.reshape(top, rows).T
    table = table[jax.random.permutation(jax.random.fold_in(own, 1), rows)]
    offset_by = jax.random.randint(jax.random.fold_in(own, 2), (rows, 1), 0, top)
    return jnp.take_along_axis(table, (jnp.arange(top)[None, :] + offset_by) % top, axis=1)


def portions_of(number_of, total, most, skew, full):
    portions = [(1 << 20) // math.isqrt(grade ** skew) + 1 for grade in range(1, number_of + 1)]
    largest = most if full else min(most, max(-(-total // number_of), total * portions[0] // sum(portions)))
    least = 1 if total - largest >= number_of - 1 else 0
    given, surplus = [largest] + [least] * (number_of - 1), total - largest - least * (number_of - 1)
    while surplus > 0:
        free = [i for i in range(1, number_of) if given[i] < largest] or [i for i in range(1, number_of) if given[i] < most]
        pool, budget = sum([portions[i] for i in free]), surplus
        for i in free:
            more = min(most - given[i], max(1, budget * portions[i] // pool), surplus)
            given[i] = given[i] + more
            surplus = surplus - more
    return np.array(given)


def setup_inputs(seed: int = 0, part: int = 0) -> dict:
    key_of = jax.random.split(jax.random.key(seed), 10)
    own_keys = jax.random.split(jax.random.fold_in(key_of[9], part), 10)
    kv_store = draw_kv_store(jax.random.fold_in(jax.random.fold_in(key_of[9], part), 71), part)
    queries = draw_queries(jax.random.fold_in(jax.random.fold_in(key_of[9], part), 71), part)
    step_kv = draw_step_kv(jax.random.fold_in(jax.random.fold_in(key_of[9], part), 71), part)
    suffix_pages = draw_suffix_pages(jax.random.fold_in(jax.random.fold_in(key_of[9], part), 71), part)
    suffix_len = draw_suffix_len(jax.random.fold_in(jax.random.fold_in(key_of[9], part), 71), part)
    owner_keys = jax.random.split(jax.random.fold_in(own_keys[5], 1), REQUESTS // REQ_DEV)
    owner_turns = jax.random.permutation(jax.random.fold_in(own_keys[5], 3), REQUESTS // REQ_DEV)
    owner = jax.vmap(lambda own, number: routed_block(jax.random.fold_in(own_keys[5], 2), own, number, REQ_DEV, N_SEQ, 1, CAP, 2))(owner_keys, owner_turns).reshape((REQUESTS, 1))
    parent_id = plant(jax.random.randint(own_keys[6], (REQUESTS,), 0, PARENTS), jax.random.fold_in(own_keys[6], 1), 0, PARENTS - 1).astype(jnp.int32)
    parent_pages = draw_parent_pages(jax.random.fold_in(jax.random.fold_in(key_of[9], part), 71), part)
    parent_len = draw_parent_len(jax.random.fold_in(jax.random.fold_in(key_of[9], part), 71), part)
    return dict(kv_store=kv_store, queries=queries, step_kv=step_kv, suffix_pages=suffix_pages, suffix_len=suffix_len, owner=owner, parent_id=parent_id, parent_pages=parent_pages, parent_len=parent_len)


MASKED_SCORE = -1e30


def heads_of(kv_rows):
    key_width = KV_HEADS * HEAD_DIM
    shape_head = kv_rows.shape[:-1] + (KV_HEADS, HEAD_DIM)
    return kv_rows[..., :key_width].reshape(shape_head), kv_rows[..., key_width:].reshape(shape_head)


def attend(query_rows, kv_rows, keep_mask):
    request_count = query_rows.shape[0]
    query_heads = query_rows.astype(jnp.float32).reshape(request_count, 2, KV_HEADS, GROUP, HEAD_DIM)
    key_rows, value_rows = heads_of(kv_rows.astype(jnp.float32))
    scores = jnp.einsum("rtgqh,rugh->rtgqu", query_heads, key_rows, precision=lax.Precision.HIGHEST) * HEAD_DIM ** -0.5
    scores = jnp.where(keep_mask[:, :, None, None, :], scores, MASKED_SCORE)
    row_max = jnp.max(scores, axis=-1, keepdims=True)
    exp_terms = jnp.exp(scores - row_max)
    row_total = jnp.sum(exp_terms, axis=-1)
    weights = lax.optimization_barrier(exp_terms.astype(jnp.bfloat16)).astype(jnp.float32)
    blended = jnp.einsum("rtgqu,rugh->rtgqh", weights, value_rows, precision=lax.Precision.HIGHEST)
    blended = blended / row_total[..., None]
    return blended.reshape(request_count, 2, -1).astype(jnp.bfloat16)


def reference(kv_store, queries, step_kv, suffix_pages, suffix_len, owner, parent_id, parent_pages, parent_len):
    page_span = PAGE * KVW
    fresh_store = kv_store[0].reshape(N_SEQ, STORE_PAGES, page_span)
    parent_store = kv_store[1].reshape(N_SEQ, STORE_PAGES, page_span)
    device = (jnp.arange(REQUESTS, dtype=jnp.int32) // REQ_DEV).astype(jnp.int32)
    suffix = fresh_store[device[:, None], suffix_pages].reshape(REQUESTS, SUF, KVW)
    positions = jnp.arange(SUF, dtype=jnp.int32)
    last_seen = suffix_len[:, None] - 2 + jnp.arange(2, dtype=jnp.int32)[None, :]
    keep_prefill = positions[None, None, :] <= last_seen[:, :, None]
    prefilled = attend(queries[0], suffix, keep_prefill)

    def one_device(device_index):
        first_row = (device_index * REQ_DEV).astype(jnp.int32)

        def take_rows(array):
            return lax.dynamic_slice_in_dim(array, first_row, REQ_DEV, 0)

        owner_seq = take_rows(owner)[:, 0]
        parent_slot = owner_seq * PARENTS + take_rows(parent_id)
        page_table = parent_pages[parent_slot]
        context = parent_store[owner_seq[:, None], page_table].reshape(REQ_DEV, PCTX, KVW)
        key_rows = jnp.concatenate([context, take_rows(suffix), take_rows(step_kv)], axis=1)
        keep_parent = jnp.arange(PCTX, dtype=jnp.int32)[None, :] < parent_len[parent_slot][:, None]
        keep_suffix = positions[None, :] < take_rows(suffix_len)[:, None]
        keep_step = jnp.arange(2, dtype=jnp.int32)[None, :] <= jnp.arange(2, dtype=jnp.int32)[:, None]
        keep_mask = jnp.concatenate([
            jnp.broadcast_to(keep_parent[:, None, :], (REQ_DEV, 2, PCTX)),
            jnp.broadcast_to(keep_suffix[:, None, :], (REQ_DEV, 2, SUF)),
            jnp.broadcast_to(keep_step[None, :, :], (REQ_DEV, 2, 2))], axis=2)
        return attend(take_rows(queries[1]), key_rows, keep_mask)

    decoded = lax.map(one_device, jnp.arange(N_SEQ, dtype=jnp.int32)).reshape(REQUESTS, 2, QW)
    return jnp.stack([prefilled, decoded])
```

```python
import functools

import jax
import jax.numpy as jnp
from jax import lax
from jax.experimental import pallas as pl
from jax.experimental.pallas import tpu as pltpu
from jax.sharding import PartitionSpec as P

HEAD_DIM = 128
KV_HEADS = 4
GROUP = 8
PAGE = 16
LANES = 128
CHUNK = 64

MASKED_SCORE = -1e30
MESH = pl.DeviceIdType.MESH


def iota(shape, dim):
    return lax.broadcasted_iota(jnp.int32, shape, dim)


def spread(index, scalars):
    out = jnp.zeros(index.shape, jnp.int32)
    for i, scalar in enumerate(scalars):
        out = jnp.where(index == i, scalar, out)
    return out


def kernel(
    n_seq,
    cap,
    owner,
    parent_id,
    suffix_len,
    suffix_pages,
    parent_pages,
    parent_len,
    q_ref,
    kv_ref,
    step_ref,
    out_ref,
    slots,
    arrived,
    work,
    rows_meta,
    key_meta,
    full,
    stats,
    ret_send,
    ret_stat_send,
    ret,
    ret_stat,
    partner_q,
    partner_o,
    partner_stat,
    send_sem,
    recv_sem,
    osend_sem,
    orecv_sem,
    ssend_sem,
    srecv_sem,
    psend_sem,
    precv_sem,
):
    role = lax.axis_index("role")
    me = lax.axis_index("seq")
    requests = owner.shape[0]
    tokens, q_width = q_ref.shape
    per_peer = 2 * cap
    slot_rows = n_seq * per_peer
    key_count = kv_ref.shape[0]
    key_width = KV_HEADS * HEAD_DIM
    scale = HEAD_DIM ** (-0.5)
    partner = {"role": 1 - role}
    on_decode = role == 1
    on_prefill = role == 0

    def peer_at(step):
        return lax.rem(me + step, n_seq)

    barrier = pltpu.get_barrier_semaphore()
    pl.semaphore_signal(barrier, inc=1, device_id=partner, device_id_type=MESH)

    @pl.when(on_decode)
    def _():
        for step in range(1, n_seq):
            pl.semaphore_signal(
                barrier, inc=1, device_id={"seq": peer_at(step)}, device_id_type=MESH
            )
        pl.semaphore_wait(barrier, n_seq)

    @pl.when(on_prefill)
    def _():
        pl.semaphore_wait(barrier, 1)

    def remote(src, dst, ssem, rsem, device):
        return pltpu.make_async_remote_copy(
            src_ref=src,
            dst_ref=dst,
            send_sem=ssem,
            recv_sem=rsem,
            device_id=device,
            device_id_type=MESH,
        )

    q_to_partner = remote(q_ref, partner_q, psend_sem.at[0], precv_sem.at[0], partner)
    o_to_partner = remote(
        full.at[pl.ds(tokens, tokens)], partner_o, psend_sem.at[1], precv_sem.at[1], partner
    )
    s_to_partner = remote(
        stats.at[pl.ds(tokens, tokens)], partner_stat, psend_sem.at[2], precv_sem.at[2], partner
    )

    def slots_to(peer, mine):
        return remote(
            slots.at[peer], arrived.at[mine], send_sem.at[peer], recv_sem.at[mine], {"seq": peer}
        )

    def out_to(peer, mine):
        return remote(
            ret_send.at[peer], ret.at[mine], osend_sem.at[peer], orecv_sem.at[mine], {"seq": peer}
        )

    def stat_to(peer, mine):
        return remote(
            ret_stat_send.at[peer],
            ret_stat.at[mine],
            ssend_sem.at[peer],
            srecv_sem.at[mine],
            {"seq": peer},
        )

    owners = [owner[r, 0] for r in range(requests)]
    places = []
    for r in range(requests):
        rank = jnp.int32(0)
        for e in range(r):
            rank = rank + jnp.where(owners[e] == owners[r], 1, 0)
        places.append(owners[r] * cap + rank)
    lengths = [suffix_len[r] for r in range(requests)]
    parents = [parent_id[r] for r in range(requests)]

    @pl.when(on_decode)
    def _():
        q_to_partner.start()
        col = iota((1, tokens), 1)
        target = 2 * spread(col >> 1, places) + (col & 1)
        pick = jnp.where(iota((slot_rows, tokens), 0) == target, 1.0, 0.0).astype(jnp.bfloat16)
        tok = iota((tokens, LANES), 0) >> 1
        pid = spread(tok, parents).astype(jnp.float32).astype(jnp.bfloat16)
        pid_slots = jnp.dot(pick, pid, preferred_element_type=jnp.float32)
        for d in range(n_seq):
            slots[d, :, q_width:] = pid_slots[d * per_peer : (d + 1) * per_peer].astype(
                jnp.bfloat16
            )
        block = 8 * LANES
        for c in range(q_width // block):
            part = jnp.dot(
                pick, q_ref[:, c * block : (c + 1) * block], preferred_element_type=jnp.float32
            )
            for d in range(n_seq):
                slots[d, :, c * block : (c + 1) * block] = part[
                    d * per_peer : (d + 1) * per_peer
                ].astype(jnp.bfloat16)
        for step in range(1, n_seq):
            slots_to(peer_at(step), me).start()

    lane_page = iota((1, key_count), 1) // PAGE
    group_row = jnp.zeros((1, key_count), jnp.int32)
    base_row = jnp.zeros((1, key_count), jnp.int32)
    suf_pages = suffix_pages.shape[1]
    par_pages = parent_pages.shape[1]
    for j in range(key_count // PAGE):
        page = jnp.where(
            on_prefill,
            suffix_pages[j // suf_pages, j % suf_pages],
            parent_pages[j // par_pages, j % par_pages],
        )
        here = lane_page == page
        group_row = jnp.where(here, jnp.where(on_prefill, j // suf_pages, j // par_pages), group_row)
        base_row = jnp.where(
            here, jnp.where(on_prefill, j % suf_pages, j % par_pages) * PAGE, base_row
        )
    pos_row = base_row + (iota((1, key_count), 1) & (PAGE - 1))
    key_meta[0:1, :] = group_row
    key_meta[1:2, :] = pos_row

    @pl.when(on_prefill)
    def _():
        row = iota((2 * tokens, LANES), 0)
        late = row >= tokens
        request = jnp.where(late, row - tokens, row) >> 1
        turn = row & 1
        length = spread(request, lengths)
        rows_meta[0, 0 : 2 * tokens] = request
        rows_meta[1, 0 : 2 * tokens] = jnp.where(late, length, length - 1 + turn)
        rows_meta[2, 0 : 2 * tokens] = jnp.where(late, turn + 1, 0)
        work[0:tokens] = q_ref[...].astype(jnp.float32)
        q_to_partner.wait_recv()
        work[tokens : 2 * tokens] = partner_q[...].astype(jnp.float32)

    @pl.when(on_decode)
    def _():
        arrived[pl.ds(me, 1)] = slots[pl.ds(me, 1)]
        for step in range(1, n_seq):
            slots_to(me, peer_at(step)).wait_recv()
        cut = [parent_len[a] for a in range(parent_len.shape[0])]
        for s in range(n_seq):
            rows = slice(s * per_peer, (s + 1) * per_peer)
            work[rows, :] = arrived[s, :, :q_width].astype(jnp.float32)
            group = arrived[s, :, q_width:].astype(jnp.float32).astype(jnp.int32)
            rows_meta[0, rows] = group
            rows_meta[1, rows] = spread(group, cut)
            rows_meta[2, rows] = jnp.zeros_like(group)

    def attend(c):
        first = c * CHUNK
        if not isinstance(c, int):
            first = pl.multiple_of(first, CHUNK)
        rows = pl.ds(first, CHUNK)
        group = rows_meta[0, rows][:, 0:1]
        limit = rows_meta[1, rows][:, 0:1]
        step_limit = rows_meta[2, rows][:, 0:1]
        keep = (key_meta[0:1, :] == group) & (key_meta[1:2, :] < limit)
        bias = jnp.where(keep, 0.0, MASKED_SCORE)
        step_key = iota((CHUNK, tokens), 1)
        step_keep = ((step_key >> 1) == group) & ((step_key & 1) < step_limit)
        step_bias = jnp.where(step_keep, 0.0, MASKED_SCORE)
        bias = jnp.concatenate([bias] * GROUP, axis=0)
        step_bias = jnp.concatenate([step_bias] * GROUP, axis=0)
        lane = iota((CHUNK, LANES), 1)
        top_all = jnp.zeros((CHUNK, LANES), jnp.float32)
        sum_all = jnp.zeros((CHUNK, LANES), jnp.float32)
        for g in range(KV_HEADS):
            heads = [
                work[rows, (g * GROUP + h) * HEAD_DIM : (g * GROUP + h + 1) * HEAD_DIM].astype(
                    jnp.bfloat16
                )
                for h in range(GROUP)
            ]
            query = jnp.concatenate(heads, axis=0)
            ks = slice(g * HEAD_DIM, (g + 1) * HEAD_DIM)
            vs = slice(key_width + g * HEAD_DIM, key_width + (g + 1) * HEAD_DIM)
            contract = (((1,), (1,)), ((), ()))
            score = (
                lax.dot_general(
                    query, kv_ref[:, ks], contract, preferred_element_type=jnp.float32
                )
                * scale
                + bias
            )
            step_score = (
                lax.dot_general(
                    query, step_ref[:, ks], contract, preferred_element_type=jnp.float32
                )
                * scale
                + step_bias
            )
            top = jnp.maximum(
                jnp.max(score, axis=1, keepdims=True), jnp.max(step_score, axis=1, keepdims=True)
            )
            term = jnp.exp(score - top)
            step_term = jnp.exp(step_score - top)
            total = jnp.sum(term, axis=1, keepdims=True) + jnp.sum(
                step_term, axis=1, keepdims=True
            )
            mixed = jnp.dot(
                term.astype(jnp.bfloat16), kv_ref[:, vs], preferred_element_type=jnp.float32
            ) + jnp.dot(
                step_term.astype(jnp.bfloat16), step_ref[:, vs], preferred_element_type=jnp.float32
            )
            mixed = mixed / total
            for h in range(GROUP):
                head = g * GROUP + h
                part = slice(h * CHUNK, (h + 1) * CHUNK)
                full[rows, head * HEAD_DIM : (head + 1) * HEAD_DIM] = mixed[part]
                top_all = jnp.where(lane == head, top[part], top_all)
                sum_all = jnp.where(lane == head, total[part], sum_all)
        stats[rows, 0:LANES] = top_all
        stats[rows, LANES:] = sum_all

    chunks = work.shape[0] // CHUNK
    if chunks == 1:
        attend(0)
    else:

        def some(c, carry):
            attend(c)
            return carry

        lax.fori_loop(
            0, jnp.where(on_prefill, pl.cdiv(2 * tokens, CHUNK), slot_rows // CHUNK), some, 0
        )

    @pl.when(on_prefill)
    def _():
        o_to_partner.start()
        s_to_partner.start()
        out_ref[...] = full[0:tokens].astype(jnp.bfloat16)
        o_to_partner.wait_send()
        s_to_partner.wait_send()

    @pl.when(on_decode)
    def _():
        for s in range(n_seq):
            rows = slice(s * per_peer, (s + 1) * per_peer)
            ret_send[s] = full[rows].astype(jnp.bfloat16)
            ret_stat_send[s] = stats[rows]
        for step in range(1, n_seq):
            peer = peer_at(step)
            stat_to(peer, me).start()
            out_to(peer, me).start()
        ret[pl.ds(me, 1)] = ret_send[pl.ds(me, 1)]
        ret_stat[pl.ds(me, 1)] = ret_stat_send[pl.ds(me, 1)]
        tok = iota((tokens, 1), 0)
        target = 2 * spread(tok >> 1, places) + (tok & 1)
        unpick = jnp.where(iota((tokens, slot_rows), 1) == target, 1.0, 0.0)
        o_to_partner.wait_recv()
        s_to_partner.wait_recv()
        for step in range(1, n_seq):
            stat_to(me, peer_at(step)).wait_recv()
            out_to(me, peer_at(step)).wait_recv()
        back = jnp.concatenate([ret_stat[s] for s in range(n_seq)], axis=0)
        far = jnp.dot(
            unpick, back, preferred_element_type=jnp.float32, precision=lax.Precision.HIGHEST
        )
        far_top, far_sum = far[:, :LANES], far[:, LANES:]
        near_top, near_sum = partner_stat[:, :LANES], partner_stat[:, LANES:]
        top = jnp.maximum(far_top, near_top)
        far_weight = far_sum * jnp.exp(far_top - top)
        near_weight = near_sum * jnp.exp(near_top - top)
        total = jnp.where(near_weight + far_weight == 0.0, 1.0, near_weight + far_weight)
        far_share = far_weight / total
        near_share = near_weight / total
        unpick = unpick.astype(jnp.bfloat16)
        for head in range(KV_HEADS * GROUP):
            part = slice(head * HEAD_DIM, (head + 1) * HEAD_DIM)
            came = jnp.concatenate(
                [ret[s, :, part].astype(jnp.float32) for s in range(n_seq)], axis=0
            ).astype(jnp.bfloat16)
            far_out = jnp.dot(unpick, came, preferred_element_type=jnp.float32)
            out_ref[:, part] = (
                far_out * far_share[:, head : head + 1]
                + partner_o[:, part] * near_share[:, head : head + 1]
            ).astype(jnp.bfloat16)
        q_to_partner.wait_send()
        for step in range(1, n_seq):
            peer = peer_at(step)
            slots_to(peer, me).wait_send()
            out_to(peer, me).wait_send()
            stat_to(peer, me).wait_send()


def local(
    kv_store, queries, step_kv, suffix_pages, suffix_len, owner, parent_id, parent_pages, parent_len
):
    n_seq = lax.axis_size("seq")
    page_store = kv_store[0]
    requests, turns, q_width = queries.shape[1:]
    tokens = requests * turns
    query_rows = queries.reshape(tokens, q_width)
    step_rows = step_kv.reshape(tokens, -1)
    cap = max(4, 2 * requests // n_seq)
    per_peer = 2 * cap
    slot_rows = n_seq * per_peer
    work_rows = max(2 * tokens, slot_rows)
    bf16, f32 = jnp.bfloat16, jnp.float32
    smem = pl.BlockSpec(memory_space=pltpu.SMEM)
    vmem = pl.BlockSpec(memory_space=pltpu.VMEM)
    dma = pltpu.SemaphoreType.DMA
    served = pl.pallas_call(
        functools.partial(kernel, n_seq, cap),
        out_shape=jax.ShapeDtypeStruct((tokens, q_width), bf16),
        in_specs=[smem] * 6 + [vmem] * 3,
        out_specs=vmem,
        scratch_shapes=[
            pltpu.VMEM((n_seq, per_peer, q_width + LANES), bf16),
            pltpu.VMEM((n_seq, per_peer, q_width + LANES), bf16),
            pltpu.VMEM((work_rows, q_width), f32),
            pltpu.VMEM((3, work_rows, LANES), jnp.int32),
            pltpu.VMEM((8, page_store.shape[0]), jnp.int32),
            pltpu.VMEM((work_rows, q_width), f32),
            pltpu.VMEM((work_rows, 2 * LANES), f32),
            pltpu.VMEM((n_seq, per_peer, q_width), bf16),
            pltpu.VMEM((n_seq, per_peer, 2 * LANES), f32),
            pltpu.VMEM((n_seq, per_peer, q_width), bf16),
            pltpu.VMEM((n_seq, per_peer, 2 * LANES), f32),
            pltpu.VMEM((tokens, q_width), bf16),
            pltpu.VMEM((tokens, q_width), f32),
            pltpu.VMEM((tokens, 2 * LANES), f32),
            dma((n_seq,)),
            dma((n_seq,)),
            dma((n_seq,)),
            dma((n_seq,)),
            dma((n_seq,)),
            dma((n_seq,)),
            dma((3,)),
            dma((3,)),
        ],
        compiler_params=pltpu.CompilerParams(
            collective_id=0, has_side_effects=True, vmem_limit_bytes=60 * 1024 * 1024
        ),
    )(
        owner,
        parent_id,
        suffix_len,
        suffix_pages,
        parent_pages,
        parent_len,
        query_rows,
        page_store,
        step_rows,
    )
    return served.reshape(1, requests, turns, q_width)


def solution(mesh):
    in_specs = (
        P("role", ("groups", "seq"), None),
        P("role", ("groups", "seq"), None, None),
        P(("groups", "seq"), None, None),
        P(("groups", "seq"), None),
        P(("groups", "seq")),
        P(("groups", "seq"), None),
        P(("groups", "seq")),
        P(("groups", "seq"), None),
        P(("groups", "seq")),
    )
    out_specs = P("role", ("groups", "seq"), None, None)
    return jax.shard_map(local, mesh=mesh, in_specs=in_specs, out_specs=out_specs, check_vma=False)
```

```python
import functools

import jax
import jax.numpy as jnp
from jax import lax
from jax.experimental import pallas as pl
from jax.experimental.pallas import tpu as pltpu
from jax.sharding import PartitionSpec as P

HEAD_DIM = 128
KV_HEADS = 4
GROUP = 8
PAGE = 16
LANES = 128

MASKED_SCORE = -1e30
MESH = pl.DeviceIdType.MESH


def iota(shape, dim):
    return lax.broadcasted_iota(jnp.int32, shape, dim)


def spread(index, scalars):
    out = jnp.zeros(index.shape, jnp.int32)
    for i, scalar in enumerate(scalars):
        out = jnp.where(index == i, scalar, out)
    return out


def kernel(
    n_seq,
    cap,
    owner,
    parent_id,
    suffix_len,
    suffix_pages,
    parent_pages,
    parent_len,
    q_hbm,
    kv_hbm,
    step_hbm,
    out_ref,
    q_ref,
    kv_ref,
    step_in,
    step_ref,
    slots,
    arrived,
    work,
    rows_meta,
    key_meta,
    full,
    stats,
    near_send,
    near_stat_send,
    ret_send,
    ret_stat_send,
    ret,
    ret_stat,
    partner_q,
    partner_o,
    partner_stat,
    load_sem,
    send_sem,
    recv_sem,
    osend_sem,
    orecv_sem,
    ssend_sem,
    srecv_sem,
    psend_sem,
    precv_sem,
):
    role = lax.axis_index("role")
    me = lax.axis_index("seq")
    requests, turns, q_width = q_ref.shape
    tokens = requests * turns
    per_peer = 2 * cap
    slot_rows = n_seq * per_peer
    chunk = 2 * per_peer
    chunk_requests = chunk // turns
    near_chunks = tokens // chunk
    key_count = kv_ref.shape[0]
    key_width = KV_HEADS * HEAD_DIM
    scale = HEAD_DIM ** (-0.5)
    partner = {"role": 1 - role}
    on_decode = role == 1
    on_prefill = role == 0
    heads_all = KV_HEADS * GROUP

    def peer_at(step):
        if n_seq & (n_seq - 1):
            return lax.rem(me + step, n_seq)
        peer = 0
        bit = 1
        while bit < n_seq:
            peer = peer + bit * (((me // bit) % 2 + (step // bit) % 2) % 2)
            bit *= 2
        return peer

    load_q = pltpu.make_async_copy(q_hbm, q_ref, load_sem.at[0])
    load_step = pltpu.make_async_copy(step_hbm, step_in, load_sem.at[1])
    load_kv = pltpu.make_async_copy(kv_hbm, kv_ref, load_sem.at[2])
    load_q.start()
    load_step.start()
    load_kv.start()

    barrier = pltpu.get_barrier_semaphore()
    pl.semaphore_signal(barrier, inc=1, device_id=partner, device_id_type=MESH)

    @pl.when(on_decode)
    def _():
        for step in range(1, n_seq):
            pl.semaphore_signal(
                barrier, inc=1, device_id={"seq": peer_at(step)}, device_id_type=MESH
            )

    def remote(src, dst, ssem, rsem, device):
        return pltpu.make_async_remote_copy(
            src_ref=src,
            dst_ref=dst,
            send_sem=ssem,
            recv_sem=rsem,
            device_id=device,
            device_id_type=MESH,
        )

    q_to_partner = remote(q_ref, partner_q, psend_sem.at[0], precv_sem.at[0], partner)
    o_to_partner = remote(near_send, partner_o, psend_sem.at[1], precv_sem.at[1], partner)
    s_to_partner = remote(near_stat_send, partner_stat, psend_sem.at[2], precv_sem.at[2], partner)

    def slots_to(peer, mine):
        return remote(
            slots.at[peer], arrived.at[mine], send_sem.at[peer], recv_sem.at[mine], {"seq": peer}
        )

    def out_to(peer, mine):
        return remote(
            ret_send.at[peer], ret.at[mine], osend_sem.at[peer], orecv_sem.at[mine], {"seq": peer}
        )

    def stat_to(peer, mine):
        return remote(
            ret_stat_send.at[peer],
            ret_stat.at[mine],
            ssend_sem.at[peer],
            srecv_sem.at[mine],
            {"seq": peer},
        )

    owners = [owner[r] for r in range(requests)]
    places = []
    for r in range(requests):
        rank = jnp.int32(0)
        for e in range(r):
            rank = rank + jnp.where(owners[e] == owners[r], 1, 0)
        places.append(owners[r] * cap + rank)
    lengths = [suffix_len[r] for r in range(requests)]
    parents = [parent_id[r] for r in range(requests)]

    load_q.wait()

    @pl.when(on_decode)
    def _():
        col = iota((1, tokens), 1)
        target = 2 * spread(col >> 1, places) + (col & 1)
        pick = jnp.where(iota((slot_rows, tokens), 0) == target, 1.0, 0.0).astype(jnp.bfloat16)
        tok = iota((tokens, LANES), 0) >> 1
        pid = spread(tok, parents).astype(jnp.float32).astype(jnp.bfloat16)
        pid_slots = jnp.dot(pick, pid, preferred_element_type=jnp.float32)
        for d in range(n_seq):
            slots[d, :, q_width:] = pid_slots[d * per_peer : (d + 1) * per_peer].astype(
                jnp.bfloat16
            )
        block = 4 * LANES
        for c in range(q_width // block):
            lanes = slice(c * block, (c + 1) * block)
            part = jnp.dot(
                pick, q_ref[:, :, lanes].reshape(tokens, block), preferred_element_type=jnp.float32
            )
            for d in range(n_seq):
                slots[d, :, lanes] = part[d * per_peer : (d + 1) * per_peer].astype(jnp.bfloat16)
        pl.semaphore_wait(barrier, n_seq)
        q_to_partner.start()
        for step in range(n_seq - 1, 0, -1):
            slots_to(peer_at(step), me).start()
        arrived[pl.ds(me, 1)] = slots[pl.ds(me, 1)]

    @pl.when(on_prefill)
    def _():
        pl.semaphore_wait(barrier, 1)

    lane_page = iota((1, key_count), 1) // PAGE
    group_row = jnp.zeros((1, key_count), jnp.int32)
    base_row = jnp.zeros((1, key_count), jnp.int32)
    suf_pages = suffix_pages.shape[0]
    par_pages = parent_pages.shape[1]
    for j in range(key_count // PAGE):
        page = jnp.where(
            on_prefill,
            suffix_pages[j % suf_pages, j // suf_pages],
            parent_pages[j // par_pages, j % par_pages],
        )
        here = lane_page == page
        group_row = jnp.where(here, jnp.where(on_prefill, j // suf_pages, j // par_pages), group_row)
        base_row = jnp.where(
            here, jnp.where(on_prefill, j % suf_pages, j % par_pages) * PAGE, base_row
        )
    pos_row = base_row + (iota((1, key_count), 1) & (PAGE - 1))
    key_meta[0:1, :] = group_row
    key_meta[1:2, :] = pos_row
    load_step.wait()
    for c in range(step_ref.shape[1] // (4 * LANES)):
        lanes = slice(c * 4 * LANES, (c + 1) * 4 * LANES)
        step_ref[:, lanes] = step_in[:, :, lanes].reshape(tokens, 4 * LANES)
    cuts = [parent_len[a] for a in range(parent_len.shape[0])]
    load_kv.wait()

    def attend():
        group = rows_meta[0, :, 0:1]
        limit = rows_meta[1, :, 0:1]
        step_limit = rows_meta[2, :, 0:1]
        keep = (key_meta[0:1, :] == group) & (key_meta[1:2, :] < limit)
        bias = jnp.where(keep, 0.0, MASKED_SCORE)
        step_key = iota((chunk, tokens), 1)
        step_keep = ((step_key >> 1) == group) & ((step_key & 1) < step_limit)
        step_bias = jnp.where(step_keep, 0.0, MASKED_SCORE)
        bias = jnp.concatenate([bias] * GROUP, axis=0)
        step_bias = jnp.concatenate([step_bias] * GROUP, axis=0)
        lane = iota((chunk, LANES), 1)
        top_all = jnp.zeros((chunk, LANES), jnp.float32)
        sum_all = jnp.zeros((chunk, LANES), jnp.float32)
        for g in range(KV_HEADS):
            query = jnp.concatenate(
                [
                    work[:, (g * GROUP + h) * HEAD_DIM : (g * GROUP + h + 1) * HEAD_DIM]
                    for h in range(GROUP)
                ],
                axis=0,
            )
            ks = slice(g * HEAD_DIM, (g + 1) * HEAD_DIM)
            vs = slice(key_width + g * HEAD_DIM, key_width + (g + 1) * HEAD_DIM)
            contract = (((1,), (1,)), ((), ()))
            score = (
                lax.dot_general(
                    query, kv_ref[:, ks], contract, preferred_element_type=jnp.float32
                )
                * scale
                + bias
            )
            step_score = (
                lax.dot_general(
                    query, step_ref[:, ks], contract, preferred_element_type=jnp.float32
                )
                * scale
                + step_bias
            )
            top = jnp.maximum(
                jnp.max(score, axis=1, keepdims=True), jnp.max(step_score, axis=1, keepdims=True)
            )
            term = jnp.exp(score - top)
            step_term = jnp.exp(step_score - top)
            total = jnp.sum(term, axis=1, keepdims=True) + jnp.sum(
                step_term, axis=1, keepdims=True
            )
            mixed = jnp.dot(
                term.astype(jnp.bfloat16), kv_ref[:, vs], preferred_element_type=jnp.float32
            ) + jnp.dot(
                step_term.astype(jnp.bfloat16), step_ref[:, vs], preferred_element_type=jnp.float32
            )
            mixed = mixed / total
            for h in range(GROUP):
                head = g * GROUP + h
                part = slice(h * chunk, (h + 1) * chunk)
                full[:, head * HEAD_DIM : (head + 1) * HEAD_DIM] = mixed[part]
                top_all = jnp.where(lane == head, top[part], top_all)
                sum_all = jnp.where(lane == head, total[part], sum_all)
        stats[:, 0:LANES] = top_all
        stats[:, LANES:] = sum_all

    def turn_of(c, carry):
        late = c >= near_chunks
        block = jnp.where(late, c - near_chunks, c)
        first_request = block * chunk_requests
        steps = (n_seq - 1 - 2 * c, n_seq - 2 - 2 * c)

        @pl.when(on_prefill)
        def _():
            row = iota((chunk, LANES), 0)
            request = first_request + (row >> 1)
            turn = row & 1
            length = spread(request, lengths)
            rows_meta[0] = request
            rows_meta[1] = jnp.where(late, length, length - 1 + turn)
            rows_meta[2] = jnp.where(late, turn + 1, 0)

            @pl.when(c == near_chunks)
            def _():
                q_to_partner.wait_recv()

            @pl.when(late)
            def _():
                for h in range(heads_all):
                    part = slice(h * HEAD_DIM, (h + 1) * HEAD_DIM)
                    work[:, part] = partner_q[
                        pl.ds(first_request, chunk_requests), :, part
                    ].reshape(chunk, HEAD_DIM)

            @pl.when(jnp.logical_not(late))
            def _():
                for h in range(heads_all):
                    part = slice(h * HEAD_DIM, (h + 1) * HEAD_DIM)
                    work[:, part] = q_ref[pl.ds(first_request, chunk_requests), :, part].reshape(
                        chunk, HEAD_DIM
                    )

        @pl.when(on_decode)
        def _():
            for i, step in enumerate(steps):
                peer = peer_at(step)

                @pl.when(step > 0)
                def _():
                    slots_to(me, peer).wait_recv()

            first, second = peer_at(steps[0]), peer_at(steps[1])
            for h in range(heads_all):
                part = slice(h * HEAD_DIM, (h + 1) * HEAD_DIM)
                work[:, part] = jnp.concatenate(
                    [
                        arrived[first, :, part].astype(jnp.float32),
                        arrived[second, :, part].astype(jnp.float32),
                    ],
                    axis=0,
                ).astype(jnp.bfloat16)
            group = jnp.concatenate(
                [
                    arrived[first, :, q_width:].astype(jnp.float32),
                    arrived[second, :, q_width:].astype(jnp.float32),
                ],
                axis=0,
            ).astype(jnp.int32)
            rows_meta[0] = group
            rows_meta[1] = spread(group, cuts)
            rows_meta[2] = jnp.zeros_like(group)

        attend()

        @pl.when(on_prefill)
        def _():
            @pl.when(late)
            def _():
                rows = pl.ds(pl.multiple_of(block * chunk, chunk), chunk)
                near_send[rows, :] = full[...]
                near_stat_send[rows, :] = stats[...]

            @pl.when(jnp.logical_not(late))
            def _():
                for h in range(heads_all):
                    part = slice(h * HEAD_DIM, (h + 1) * HEAD_DIM)
                    out_ref[pl.ds(first_request, chunk_requests), :, part] = (
                        full[:, part].astype(jnp.bfloat16).reshape(chunk_requests, turns, HEAD_DIM)
                    )

        @pl.when(on_decode)
        def _():
            for i, step in enumerate(steps):
                peer = peer_at(step)
                rows = slice(i * per_peer, (i + 1) * per_peer)
                ret_send[peer] = full[rows].astype(jnp.bfloat16)
                ret_stat_send[peer] = stats[rows]

                @pl.when(step > 0)
                def _():
                    stat_to(peer, me).start()
                    out_to(peer, me).start()

        return carry

    lax.fori_loop(0, jnp.where(on_prefill, 2 * near_chunks, n_seq // 2), turn_of, 0)

    @pl.when(on_prefill)
    def _():
        s_to_partner.start()
        o_to_partner.start()
        s_to_partner.wait_send()
        o_to_partner.wait_send()

    @pl.when(on_decode)
    def _():
        ret[pl.ds(me, 1)] = ret_send[pl.ds(me, 1)]
        ret_stat[pl.ds(me, 1)] = ret_stat_send[pl.ds(me, 1)]
        tok = iota((tokens, 1), 0)
        target = 2 * spread(tok >> 1, places) + (tok & 1)
        unpick = jnp.where(iota((tokens, slot_rows), 1) == target, 1.0, 0.0)
        o_to_partner.wait_recv()
        s_to_partner.wait_recv()
        for step in range(n_seq - 1, 0, -1):
            stat_to(me, peer_at(step)).wait_recv()
            out_to(me, peer_at(step)).wait_recv()
        back = jnp.concatenate([ret_stat[s] for s in range(n_seq)], axis=0)
        far = jnp.dot(
            unpick, back, preferred_element_type=jnp.float32, precision=lax.Precision.HIGHEST
        )
        far_top, far_sum = far[:, :LANES], far[:, LANES:]
        near_top, near_sum = partner_stat[:, :LANES], partner_stat[:, LANES:]
        top = jnp.maximum(far_top, near_top)
        far_weight = far_sum * jnp.exp(far_top - top)
        near_weight = near_sum * jnp.exp(near_top - top)
        total = jnp.where(near_weight + far_weight == 0.0, 1.0, near_weight + far_weight)
        far_share = far_weight / total
        near_share = near_weight / total
        unpick = unpick.astype(jnp.bfloat16)
        for head in range(heads_all):
            part = slice(head * HEAD_DIM, (head + 1) * HEAD_DIM)
            came = jnp.concatenate(
                [ret[s, :, part].astype(jnp.float32) for s in range(n_seq)], axis=0
            ).astype(jnp.bfloat16)
            far_out = jnp.dot(unpick, came, preferred_element_type=jnp.float32)
            out_ref[:, :, part] = (
                (
                    far_out * far_share[:, head : head + 1]
                    + partner_o[:, part] * near_share[:, head : head + 1]
                )
                .astype(jnp.bfloat16)
                .reshape(requests, turns, HEAD_DIM)
            )
        q_to_partner.wait_send()
        for step in range(1, n_seq):
            peer = peer_at(step)
            slots_to(peer, me).wait_send()
            out_to(peer, me).wait_send()
            stat_to(peer, me).wait_send()


def local(
    kv_store, queries, step_kv, suffix_pages, suffix_len, owner, parent_id, parent_pages, parent_len
):
    n_seq = lax.axis_size("seq")
    page_store = kv_store[0]
    requests, turns, q_width = queries.shape[1:]
    tokens = requests * turns
    cap = max(4, 2 * requests // n_seq)
    per_peer = 2 * cap
    chunk = 2 * per_peer
    bf16, f32 = jnp.bfloat16, jnp.float32
    smem = pl.BlockSpec(memory_space=pltpu.SMEM)
    vmem = pl.BlockSpec(memory_space=pltpu.VMEM)
    hbm = pl.BlockSpec(memory_space=pl.ANY)
    dma = pltpu.SemaphoreType.DMA
    served = pl.pallas_call(
        functools.partial(kernel, n_seq, cap),
        out_shape=jax.ShapeDtypeStruct((requests, turns, q_width), bf16),
        in_specs=[smem] * 6 + [hbm] * 3,
        out_specs=vmem,
        scratch_shapes=[
            pltpu.VMEM((requests, turns, q_width), bf16),
            pltpu.VMEM(page_store.shape, bf16),
            pltpu.VMEM(step_kv.shape, bf16),
            pltpu.VMEM((tokens, step_kv.shape[2]), bf16),
            pltpu.VMEM((n_seq, per_peer, q_width + LANES), bf16),
            pltpu.VMEM((n_seq, per_peer, q_width + LANES), bf16),
            pltpu.VMEM((chunk, q_width), bf16),
            pltpu.VMEM((3, chunk, LANES), jnp.int32),
            pltpu.VMEM((8, page_store.shape[0]), jnp.int32),
            pltpu.VMEM((chunk, q_width), f32),
            pltpu.VMEM((chunk, 2 * LANES), f32),
            pltpu.VMEM((tokens, q_width), f32),
            pltpu.VMEM((tokens, 2 * LANES), f32),
            pltpu.VMEM((n_seq, per_peer, q_width), bf16),
            pltpu.VMEM((n_seq, per_peer, 2 * LANES), f32),
            pltpu.VMEM((n_seq, per_peer, q_width), bf16),
            pltpu.VMEM((n_seq, per_peer, 2 * LANES), f32),
            pltpu.VMEM((requests, turns, q_width), bf16),
            pltpu.VMEM((tokens, q_width), f32),
            pltpu.VMEM((tokens, 2 * LANES), f32),
            dma((3,)),
            dma((n_seq,)),
            dma((n_seq,)),
            dma((n_seq,)),
            dma((n_seq,)),
            dma((n_seq,)),
            dma((n_seq,)),
            dma((3,)),
            dma((3,)),
        ],
        compiler_params=pltpu.CompilerParams(
            collective_id=0, has_side_effects=True, vmem_limit_bytes=60 * 1024 * 1024
        ),
    )(
        owner.reshape(-1),
        parent_id,
        suffix_len,
        suffix_pages.T,
        parent_pages,
        parent_len,
        queries[0],
        page_store,
        step_kv,
    )
    return served[None]


def solution(mesh):
    in_specs = (
        P("role", ("groups", "seq"), None),
        P("role", ("groups", "seq"), None, None),
        P(("groups", "seq"), None, None),
        P(("groups", "seq"), None),
        P(("groups", "seq")),
        P(("groups", "seq"), None),
        P(("groups", "seq")),
        P(("groups", "seq"), None),
        P(("groups", "seq")),
    )
    out_specs = P("role", ("groups", "seq"), None, None)
    return jax.shard_map(local, mesh=mesh, in_specs=in_specs, out_specs=out_specs, check_vma=False)
```

```python
import functools

import jax
import jax.numpy as jnp
from jax import lax
from jax.experimental import pallas as pl
from jax.experimental.pallas import tpu as pltpu
from jax.sharding import PartitionSpec as P

HEAD_DIM = 128
KV_HEADS = 4
GROUP = 8
PAGE = 16
LANES = 128

MASKED_SCORE = -1e30
MESH = pl.DeviceIdType.MESH


def iota(shape, dim):
    return lax.broadcasted_iota(jnp.int32, shape, dim)


def spread(index, scalars):
    out = jnp.zeros(index.shape, jnp.int32)
    for i, scalar in enumerate(scalars):
        out = jnp.where(index == i, scalar, out)
    return out


def kernel(
    n_seq,
    cap,
    owner_hbm,
    parent_id_hbm,
    suffix_len_hbm,
    suffix_pages_hbm,
    parent_pages_hbm,
    parent_len_hbm,
    q_hbm,
    kv_hbm,
    step_hbm,
    out_ref,
    owner,
    parent_id,
    suffix_len,
    suffix_pages,
    parent_pages,
    parent_len,
    q_ref,
    kv_ref,
    step_in,
    step_ref,
    slots,
    arrived,
    key_meta,
    near_send,
    near_stat_send,
    ret_send,
    ret_stat_send,
    ret,
    ret_stat,
    partner_q,
    partner_o,
    partner_stat,
    load_sem,
    send_sem,
    recv_sem,
    osend_sem,
    orecv_sem,
    ssend_sem,
    srecv_sem,
    psend_sem,
    precv_sem,
):
    role = lax.axis_index("role")
    me = lax.axis_index("seq")
    requests, turns, q_width = q_ref.shape
    tokens = requests * turns
    per_peer = 2 * cap
    slot_rows = n_seq * per_peer
    key_count = kv_ref.shape[0]
    key_width = KV_HEADS * HEAD_DIM
    scale = HEAD_DIM ** (-0.5)
    partner = {"role": 1 - role}
    on_decode = role == 1
    on_prefill = role == 0
    heads_all = KV_HEADS * GROUP

    bits = [(me // 2**b) % 2 for b in range(n_seq.bit_length() - 1)]

    def peer_at(step):
        if n_seq & (n_seq - 1):
            return lax.rem(me + step, n_seq)
        peer = me
        for b, mine in enumerate(bits):
            if isinstance(step, int):
                if (step >> b) & 1:
                    peer = peer + 2**b * (1 - 2 * mine)
            else:
                peer = peer + 2**b * (1 - 2 * mine) * ((step // 2**b) % 2)
        return peer

    load_q = pltpu.make_async_copy(q_hbm, q_ref, load_sem.at[0])
    load_step = pltpu.make_async_copy(step_hbm, step_in, load_sem.at[1])
    load_kv = pltpu.make_async_copy(kv_hbm, kv_ref, load_sem.at[2])
    tables = [
        pltpu.make_async_copy(src, dst, load_sem.at[3 + i])
        for i, (src, dst) in enumerate(
            (
                (owner_hbm, owner),
                (parent_id_hbm, parent_id),
                (suffix_len_hbm, suffix_len),
                (suffix_pages_hbm, suffix_pages),
                (parent_pages_hbm, parent_pages),
                (parent_len_hbm, parent_len),
            )
        )
    ]
    load_q.start()
    for table in tables:
        table.start()
    load_step.start()
    load_kv.start()

    barrier = pltpu.get_barrier_semaphore()
    pl.semaphore_signal(barrier, inc=1, device_id=partner, device_id_type=MESH)

    @pl.when(on_decode)
    def _():
        for step in range(1, n_seq):
            pl.semaphore_signal(
                barrier, inc=1, device_id={"seq": peer_at(step)}, device_id_type=MESH
            )

    def remote(src, dst, ssem, rsem, device):
        return pltpu.make_async_remote_copy(
            src_ref=src,
            dst_ref=dst,
            send_sem=ssem,
            recv_sem=rsem,
            device_id=device,
            device_id_type=MESH,
        )

    q_to_partner = remote(q_ref, partner_q, psend_sem.at[0], precv_sem.at[0], partner)
    o_to_partner = remote(near_send, partner_o, psend_sem.at[1], precv_sem.at[1], partner)
    s_to_partner = remote(near_stat_send, partner_stat, psend_sem.at[2], precv_sem.at[2], partner)

    def slots_to(peer, mine):
        return remote(
            slots.at[peer], arrived.at[mine], send_sem.at[peer], recv_sem.at[mine], {"seq": peer}
        )

    def out_to(peer, mine):
        return remote(
            ret_send.at[peer], ret.at[mine], osend_sem.at[peer], orecv_sem.at[mine], {"seq": peer}
        )

    def stat_to(peer, mine):
        return remote(
            ret_stat_send.at[peer],
            ret_stat.at[mine],
            ssend_sem.at[peer],
            srecv_sem.at[mine],
            {"seq": peer},
        )

    for table in tables:
        table.wait()
    owners = [owner[r] for r in range(requests)]
    places = []
    for r in range(requests):
        rank = jnp.int32(0)
        for e in range(r):
            rank = rank + jnp.where(owners[e] == owners[r], 1, 0)
        places.append(owners[r] * cap + rank)
    lengths = [suffix_len[r] for r in range(requests)]
    parents = [parent_id[r] for r in range(requests)]

    load_q.wait()

    @pl.when(on_decode)
    def _():
        col = iota((1, tokens), 1)
        target = 2 * spread(col >> 1, places) + (col & 1)
        pick = jnp.where(iota((slot_rows, tokens), 0) == target, 1.0, 0.0).astype(jnp.bfloat16)
        tok = iota((tokens, LANES), 0) >> 1
        pid = spread(tok, parents).astype(jnp.float32).astype(jnp.bfloat16)
        pid_slots = jnp.dot(pick, pid, preferred_element_type=jnp.float32)
        for d in range(n_seq):
            slots[d, :, q_width:] = pid_slots[d * per_peer : (d + 1) * per_peer].astype(
                jnp.bfloat16
            )
        block = 4 * LANES
        for c in range(q_width // block):
            lanes = slice(c * block, (c + 1) * block)
            part = jnp.dot(
                pick, q_ref[:, :, lanes].reshape(tokens, block), preferred_element_type=jnp.float32
            )
            for d in range(n_seq):
                slots[d, :, lanes] = part[d * per_peer : (d + 1) * per_peer].astype(jnp.bfloat16)
        pl.semaphore_wait(barrier, n_seq)
        q_to_partner.start()
        for step in range(n_seq - 1, 0, -1):
            slots_to(peer_at(step), me).start()
        arrived[pl.ds(me, 1)] = slots[pl.ds(me, 1)]

    @pl.when(on_prefill)
    def _():
        pl.semaphore_wait(barrier, 1)

    lane_page = iota((1, key_count), 1) // PAGE
    group_row = jnp.zeros((1, key_count), jnp.int32)
    base_row = jnp.zeros((1, key_count), jnp.int32)
    suf_pages = suffix_pages.shape[0]
    par_pages = parent_pages.shape[1]
    for j in range(key_count // PAGE):
        page = jnp.where(
            on_prefill,
            suffix_pages[j % suf_pages, j // suf_pages],
            parent_pages[j // par_pages, j % par_pages],
        )
        here = lane_page == page
        group_row = jnp.where(here, jnp.where(on_prefill, j // suf_pages, j // par_pages), group_row)
        base_row = jnp.where(
            here, jnp.where(on_prefill, j % suf_pages, j % par_pages) * PAGE, base_row
        )
    pos_row = base_row + (iota((1, key_count), 1) & (PAGE - 1))
    key_meta[0:1, :] = group_row
    key_meta[1:2, :] = pos_row
    load_step.wait()
    for c in range(step_ref.shape[1] // (4 * LANES)):
        lanes = slice(c * 4 * LANES, (c + 1) * 4 * LANES)
        step_ref[:, lanes] = step_in[:, :, lanes].reshape(tokens, 4 * LANES)
    cuts = [parent_len[a] for a in range(parent_len.shape[0])]
    load_kv.wait()

    def attend(get, put, group, limit, step_limit):
        rows = group.shape[0]
        keep = (key_meta[0:1, :] == group) & (key_meta[1:2, :] < limit)
        bias = jnp.where(keep, 0.0, MASKED_SCORE)[None]
        if step_limit is not None:
            step_key = iota((rows, tokens), 1)
            step_keep = ((step_key >> 1) == group) & ((step_key & 1) < step_limit)
            step_bias = jnp.where(step_keep, 0.0, MASKED_SCORE)[None]
        lane = iota((rows, LANES), 1)
        top_all = jnp.zeros((rows, LANES), jnp.float32)
        sum_all = jnp.zeros((rows, LANES), jnp.float32)
        contract = (((1,), (1,)), ((), ()))

        def scores(query, keys, add):
            found = lax.dot_general(query, keys, contract, preferred_element_type=jnp.float32)
            return found.reshape(GROUP, rows, keys.shape[0]) * scale + add

        def blend(term, values):
            term = term.reshape(GROUP * rows, values.shape[0]).astype(jnp.bfloat16)
            mixed = jnp.dot(term, values, preferred_element_type=jnp.float32)
            return mixed.reshape(GROUP, rows, HEAD_DIM)

        for g in range(KV_HEADS):
            query = jnp.concatenate([get(g * GROUP + h) for h in range(GROUP)], axis=0)
            ks = slice(g * HEAD_DIM, (g + 1) * HEAD_DIM)
            vs = slice(key_width + g * HEAD_DIM, key_width + (g + 1) * HEAD_DIM)
            score = scores(query, kv_ref[:, ks], bias)
            top = jnp.max(score, axis=2, keepdims=True)
            if step_limit is not None:
                step_score = scores(query, step_ref[:, ks], step_bias)
                top = jnp.maximum(top, jnp.max(step_score, axis=2, keepdims=True))
            term = jnp.exp(score - top)
            total = jnp.sum(term, axis=2, keepdims=True)
            mixed = blend(term, kv_ref[:, vs])
            if step_limit is not None:
                step_term = jnp.exp(step_score - top)
                total = total + jnp.sum(step_term, axis=2, keepdims=True)
                mixed = mixed + blend(step_term, step_ref[:, vs])
            mixed = mixed / total
            for h in range(GROUP):
                head = g * GROUP + h
                put(head, mixed[h])
                top_all = jnp.where(lane == head, top[h], top_all)
                sum_all = jnp.where(lane == head, total[h], sum_all)
        return top_all, sum_all

    @pl.when(on_prefill)
    def _():
        row = iota((tokens, 1), 0)
        request = row >> 1
        turn = row & 1
        length = spread(request, lengths)

        def lanes_of(head):
            return slice(head * HEAD_DIM, (head + 1) * HEAD_DIM)

        def own(head):
            return q_ref[:, :, lanes_of(head)].reshape(tokens, HEAD_DIM)

        def passed(head):
            return partner_q[:, :, lanes_of(head)].reshape(tokens, HEAD_DIM)

        def serve(head, value):
            out_ref[:, lanes_of(head)] = value.astype(jnp.bfloat16)

        def keep(head, value):
            near_send[:, lanes_of(head)] = value

        q_to_partner.wait_recv()
        top, total = attend(passed, keep, request, length, turn + 1)
        near_stat_send[:, :LANES] = top
        near_stat_send[:, LANES:] = total
        o_to_partner.start()
        s_to_partner.start()
        attend(own, serve, request, length - 1 + turn, None)
        s_to_partner.wait_send()
        o_to_partner.wait_send()

    batch = min(4, n_seq)

    def answer(c):
        steps = [n_seq - 1 - batch * c - i for i in range(batch)]
        peers = [peer_at(step) for step in steps]

        def unless_own(step, action):
            if isinstance(step, int):
                if step > 0:
                    action()
            else:
                pl.when(step > 0)(action)

        for step, peer in zip(steps, peers):
            unless_own(step, lambda peer=peer: slots_to(me, peer).wait_recv())

        def gathered(lanes):
            return jnp.concatenate(
                [arrived[peer, :, lanes].astype(jnp.float32) for peer in peers], axis=0
            )

        def get(head):
            return gathered(slice(head * HEAD_DIM, (head + 1) * HEAD_DIM)).astype(jnp.bfloat16)

        def put(head, value):
            for i, peer in enumerate(peers):
                ret_send[peer, :, head * HEAD_DIM : (head + 1) * HEAD_DIM] = value[
                    i * per_peer : (i + 1) * per_peer
                ].astype(jnp.bfloat16)

        group = gathered(slice(q_width, q_width + LANES)).astype(jnp.int32)[:, 0:1]
        top, total = attend(get, put, group, spread(group, cuts), None)
        for i, peer in enumerate(peers):
            rows = slice(i * per_peer, (i + 1) * per_peer)
            ret_stat_send[peer, :, :LANES] = top[rows]
            ret_stat_send[peer, :, LANES:] = total[rows]

        def reply(peer):
            stat_to(peer, me).start()
            out_to(peer, me).start()

        for step, peer in zip(steps, peers):
            unless_own(step, lambda peer=peer: reply(peer))

    @pl.when(on_decode)
    def _():
        if n_seq // batch <= 4:
            for c in range(n_seq // batch):
                answer(c)
        else:

            def one(c, carry):
                answer(c)
                return carry

            lax.fori_loop(0, n_seq // batch, one, 0)

    @pl.when(on_decode)
    def _():
        ret[pl.ds(me, 1)] = ret_send[pl.ds(me, 1)]
        ret_stat[pl.ds(me, 1)] = ret_stat_send[pl.ds(me, 1)]
        tok = iota((tokens, 1), 0)
        target = 2 * spread(tok >> 1, places) + (tok & 1)
        unpick = jnp.where(iota((tokens, slot_rows), 1) == target, 1.0, 0.0)
        o_to_partner.wait_recv()
        s_to_partner.wait_recv()
        for step in range(n_seq - 1, 0, -1):
            stat_to(me, peer_at(step)).wait_recv()
            out_to(me, peer_at(step)).wait_recv()
        back = jnp.concatenate([ret_stat[s] for s in range(n_seq)], axis=0)
        far = jnp.dot(
            unpick, back, preferred_element_type=jnp.float32, precision=lax.Precision.HIGHEST
        )
        far_top, far_sum = far[:, :LANES], far[:, LANES:]
        near_top, near_sum = partner_stat[:, :LANES], partner_stat[:, LANES:]
        top = jnp.maximum(far_top, near_top)
        far_weight = far_sum * jnp.exp(far_top - top)
        near_weight = near_sum * jnp.exp(near_top - top)
        total = jnp.where(near_weight + far_weight == 0.0, 1.0, near_weight + far_weight)
        far_share = far_weight / total
        near_share = near_weight / total
        unpick = unpick.astype(jnp.bfloat16)
        for head in range(heads_all):
            part = slice(head * HEAD_DIM, (head + 1) * HEAD_DIM)
            came = jnp.concatenate(
                [ret[s, :, part].astype(jnp.float32) for s in range(n_seq)], axis=0
            ).astype(jnp.bfloat16)
            far_out = jnp.dot(unpick, came, preferred_element_type=jnp.float32)
            out_ref[:, part] = (
                far_out * far_share[:, head : head + 1]
                + partner_o[:, part] * near_share[:, head : head + 1]
            ).astype(jnp.bfloat16)
        q_to_partner.wait_send()
        for step in range(1, n_seq):
            peer = peer_at(step)
            slots_to(peer, me).wait_send()
            out_to(peer, me).wait_send()
            stat_to(peer, me).wait_send()


def local(
    kv_store, queries, step_kv, suffix_pages, suffix_len, owner, parent_id, parent_pages, parent_len
):
    n_seq = lax.axis_size("seq")
    page_store = kv_store[0]
    requests, turns, q_width = queries.shape[1:]
    tokens = requests * turns
    cap = max(4, 2 * requests // n_seq)
    per_peer = 2 * cap
    bf16, f32 = jnp.bfloat16, jnp.float32
    vmem = pl.BlockSpec(memory_space=pltpu.VMEM)
    hbm = pl.BlockSpec(memory_space=pl.ANY)
    dma = pltpu.SemaphoreType.DMA
    served = pl.pallas_call(
        functools.partial(kernel, n_seq, cap),
        out_shape=jax.ShapeDtypeStruct((tokens, q_width), bf16),
        in_specs=[hbm] * 9,
        out_specs=vmem,
        scratch_shapes=[
            pltpu.SMEM((requests,), jnp.int32),
            pltpu.SMEM((requests,), jnp.int32),
            pltpu.SMEM((requests,), jnp.int32),
            pltpu.SMEM(suffix_pages.shape[::-1], jnp.int32),
            pltpu.SMEM(parent_pages.shape, jnp.int32),
            pltpu.SMEM(parent_len.shape, jnp.int32),
            pltpu.VMEM((requests, turns, q_width), bf16),
            pltpu.VMEM(page_store.shape, bf16),
            pltpu.VMEM(step_kv.shape, bf16),
            pltpu.VMEM((tokens, step_kv.shape[2]), bf16),
            pltpu.VMEM((n_seq, per_peer, q_width + LANES), bf16),
            pltpu.VMEM((n_seq, per_peer, q_width + LANES), bf16),
            pltpu.VMEM((8, page_store.shape[0]), jnp.int32),
            pltpu.VMEM((tokens, q_width), f32),
            pltpu.VMEM((tokens, 2 * LANES), f32),
            pltpu.VMEM((n_seq, per_peer, q_width), bf16),
            pltpu.VMEM((n_seq, per_peer, 2 * LANES), f32),
            pltpu.VMEM((n_seq, per_peer, q_width), bf16),
            pltpu.VMEM((n_seq, per_peer, 2 * LANES), f32),
            pltpu.VMEM((requests, turns, q_width), bf16),
            pltpu.VMEM((tokens, q_width), f32),
            pltpu.VMEM((tokens, 2 * LANES), f32),
            dma((9,)),
            dma((n_seq,)),
            dma((n_seq,)),
            dma((n_seq,)),
            dma((n_seq,)),
            dma((n_seq,)),
            dma((n_seq,)),
            dma((3,)),
            dma((3,)),
        ],
        compiler_params=pltpu.CompilerParams(
            collective_id=0, has_side_effects=True, vmem_limit_bytes=60 * 1024 * 1024
        ),
    )(
        owner.reshape(-1),
        parent_id,
        suffix_len,
        suffix_pages.T,
        parent_pages,
        parent_len,
        queries[0],
        page_store,
        step_kv,
    )
    return served.reshape(1, requests, turns, q_width)


def solution(mesh):
    in_specs = (
        P("role", ("groups", "seq"), None),
        P("role", ("groups", "seq"), None, None),
        P(("groups", "seq"), None, None),
        P(("groups", "seq"), None),
        P(("groups", "seq")),
        P(("groups", "seq"), None),
        P(("groups", "seq")),
        P(("groups", "seq"), None),
        P(("groups", "seq")),
    )
    out_specs = P("role", ("groups", "seq"), None, None)
    return jax.shard_map(local, mesh=mesh, in_specs=in_specs, out_specs=out_specs, check_vma=False)
```

```python
import functools

import jax
import jax.numpy as jnp
from jax import lax
from jax.experimental import pallas as pl
from jax.experimental.pallas import tpu as pltpu
from jax.sharding import PartitionSpec as P

HEAD_DIM = 128
KV_HEADS = 4
GROUP = 8
PAGE = 16
LANES = 128

MASKED_SCORE = -1e30
MESH = pl.DeviceIdType.MESH


def iota(shape, dim):
    return lax.broadcasted_iota(jnp.int32, shape, dim)


def spread(index, scalars):
    out = jnp.zeros(index.shape, jnp.int32)
    for i, scalar in enumerate(scalars):
        out = jnp.where(index == i, scalar, out)
    return out


def kernel(
    n_seq,
    cap,
    owner_hbm,
    parent_id_hbm,
    suffix_len_hbm,
    suffix_pages_hbm,
    parent_pages_hbm,
    parent_len_hbm,
    q_hbm,
    kv_hbm,
    step_hbm,
    out_ref,
    owner,
    parent_id,
    suffix_len,
    suffix_pages,
    parent_pages,
    parent_len,
    q_ref,
    kv_ref,
    step_in,
    step_ref,
    slots,
    arrived,
    key_meta,
    slot_bias,
    far_out,
    near_send,
    near_stat_send,
    ret_send,
    ret_stat_send,
    ret,
    ret_stat,
    partner_q,
    partner_o,
    partner_stat,
    load_sem,
    send_sem,
    recv_sem,
    osend_sem,
    orecv_sem,
    ssend_sem,
    srecv_sem,
    psend_sem,
    precv_sem,
):
    role = lax.axis_index("role")
    me = lax.axis_index("seq")
    requests, turns, q_width = q_ref.shape
    tokens = requests * turns
    per_peer = 2 * cap
    slot_rows = n_seq * per_peer
    key_count = kv_ref.shape[0]
    key_width = KV_HEADS * HEAD_DIM
    scale = HEAD_DIM ** (-0.5)
    partner = {"role": 1 - role}
    on_decode = role == 1
    on_prefill = role == 0
    heads_all = KV_HEADS * GROUP
    group_width = GROUP * HEAD_DIM
    half = LANES // 2

    bits = [(me // 2**b) % 2 for b in range(n_seq.bit_length() - 1)]

    def peer_at(step):
        if n_seq & (n_seq - 1):
            return lax.rem(me + step, n_seq)
        peer = me
        for b, mine in enumerate(bits):
            if isinstance(step, int):
                if (step >> b) & 1:
                    peer = peer + 2**b * (1 - 2 * mine)
            else:
                peer = peer + 2**b * (1 - 2 * mine) * ((step // 2**b) % 2)
        return peer

    load_q = pltpu.make_async_copy(q_hbm, q_ref, load_sem.at[0])
    load_step = pltpu.make_async_copy(step_hbm, step_in, load_sem.at[1])
    load_kv = pltpu.make_async_copy(kv_hbm, kv_ref, load_sem.at[2])
    tables = [
        pltpu.make_async_copy(src, dst, load_sem.at[3 + i])
        for i, (src, dst) in enumerate(
            (
                (owner_hbm, owner),
                (parent_id_hbm, parent_id),
                (suffix_len_hbm, suffix_len),
                (suffix_pages_hbm, suffix_pages),
                (parent_pages_hbm, parent_pages),
                (parent_len_hbm, parent_len),
            )
        )
    ]
    load_q.start()
    for table in tables:
        table.start()
    load_step.start()
    load_kv.start()

    barrier = pltpu.get_barrier_semaphore()
    pl.semaphore_signal(barrier, inc=1, device_id=partner, device_id_type=MESH)

    @pl.when(on_decode)
    def _():
        for step in range(1, n_seq):
            pl.semaphore_signal(
                barrier, inc=1, device_id={"seq": peer_at(step)}, device_id_type=MESH
            )

    def remote(src, dst, ssem, rsem, device):
        return pltpu.make_async_remote_copy(
            src_ref=src,
            dst_ref=dst,
            send_sem=ssem,
            recv_sem=rsem,
            device_id=device,
            device_id_type=MESH,
        )

    q_to_partner = remote(q_ref, partner_q, psend_sem.at[0], precv_sem.at[0], partner)
    o_to_partner = remote(near_send, partner_o, psend_sem.at[1], precv_sem.at[1], partner)
    s_to_partner = remote(near_stat_send, partner_stat, psend_sem.at[2], precv_sem.at[2], partner)

    def q_lanes(g):
        first = 0 if g == 0 else LANES + g * group_width
        return slice(first, LANES + (g + 1) * group_width)

    def slots_to(peer, mine, g):
        return remote(
            slots.at[peer, :, q_lanes(g)],
            arrived.at[mine, :, q_lanes(g)],
            send_sem.at[peer, g],
            recv_sem.at[mine, g],
            {"seq": peer},
        )

    def out_to(peer, mine, g):
        lanes = slice(g * group_width, (g + 1) * group_width)
        return remote(
            ret_send.at[peer, :, lanes],
            ret.at[mine, :, lanes],
            osend_sem.at[peer, g],
            orecv_sem.at[mine, g],
            {"seq": peer},
        )

    def stat_to(peer, mine):
        return remote(
            ret_stat_send.at[peer],
            ret_stat.at[mine],
            ssend_sem.at[peer],
            srecv_sem.at[mine],
            {"seq": peer},
        )

    for table in tables:
        table.wait()
    owners = [owner[r] for r in range(requests)]
    places = []
    for r in range(requests):
        rank = jnp.int32(0)
        for e in range(r):
            rank = rank + jnp.where(owners[e] == owners[r], 1, 0)
        places.append(owners[r] * cap + rank)
    lengths = [suffix_len[r] for r in range(requests)]
    parents = [parent_id[r] for r in range(requests)]

    load_q.wait()

    @pl.when(on_decode)
    def _():
        col = iota((1, tokens), 1)
        target = 2 * spread(col >> 1, places) + (col & 1)
        pick = jnp.where(iota((slot_rows, tokens), 0) == target, 1.0, 0.0).astype(jnp.bfloat16)
        tok = iota((tokens, LANES), 0) >> 1
        pid = spread(tok, parents).astype(jnp.float32).astype(jnp.bfloat16)
        pid_slots = jnp.dot(pick, pid, preferred_element_type=jnp.float32)
        for d in range(n_seq):
            slots[d, :, :LANES] = pid_slots[d * per_peer : (d + 1) * per_peer].astype(
                jnp.bfloat16
            )
        block = 4 * LANES
        for c in range(q_width // block):
            lanes = slice(c * block, (c + 1) * block)
            part = jnp.dot(
                pick, q_ref[:, :, lanes].reshape(tokens, block), preferred_element_type=jnp.float32
            )
            for d in range(n_seq):
                slots[d, :, LANES + c * block : LANES + (c + 1) * block] = part[d * per_peer : (d + 1) * per_peer].astype(jnp.bfloat16)
        pl.semaphore_wait(barrier, n_seq)
        q_to_partner.start()
        for g in range(KV_HEADS):
            for step in range(n_seq - 1, 0, -1):
                slots_to(peer_at(step), me, g).start()
        arrived[pl.ds(me, 1)] = slots[pl.ds(me, 1)]

    @pl.when(on_prefill)
    def _():
        pl.semaphore_wait(barrier, 1)

    lane_page = iota((1, key_count), 1) // PAGE
    group_row = jnp.zeros((1, key_count), jnp.int32)
    base_row = jnp.zeros((1, key_count), jnp.int32)
    suf_pages = suffix_pages.shape[0]
    par_pages = parent_pages.shape[1]
    for j in range(key_count // PAGE):
        page = jnp.where(
            on_prefill,
            suffix_pages[j % suf_pages, j // suf_pages],
            parent_pages[j // par_pages, j % par_pages],
        )
        here = lane_page == page
        group_row = jnp.where(here, jnp.where(on_prefill, j // suf_pages, j // par_pages), group_row)
        base_row = jnp.where(
            here, jnp.where(on_prefill, j % suf_pages, j % par_pages) * PAGE, base_row
        )
    pos_row = base_row + (iota((1, key_count), 1) & (PAGE - 1))
    key_meta[0:1, :] = group_row
    key_meta[1:2, :] = pos_row
    load_step.wait()
    for c in range(step_ref.shape[1] // (4 * LANES)):
        lanes = slice(c * 4 * LANES, (c + 1) * 4 * LANES)
        step_ref[:, lanes] = step_in[:, :, lanes].reshape(tokens, 4 * LANES)
    cuts = [parent_len[a] for a in range(parent_len.shape[0])]
    load_kv.wait()

    def bias_of(group, limit):
        keep = (key_meta[0:1, :] == group) & (key_meta[1:2, :] < limit)
        return jnp.where(keep, 0.0, MASKED_SCORE)

    def attend(g, query, bias, step_bias=None):
        rows = bias.shape[0]
        ks = slice(g * HEAD_DIM, (g + 1) * HEAD_DIM)
        vs = slice(key_width + g * HEAD_DIM, key_width + (g + 1) * HEAD_DIM)
        contract = (((1,), (1,)), ((), ()))

        def scores(keys, add):
            found = lax.dot_general(query, keys, contract, preferred_element_type=jnp.float32)
            return found.reshape(GROUP, rows, keys.shape[0]) * scale + add[None]

        def blend(term, values):
            term = term.reshape(GROUP * rows, values.shape[0]).astype(jnp.bfloat16)
            mixed = jnp.dot(term, values, preferred_element_type=jnp.float32)
            return mixed.reshape(GROUP, rows, HEAD_DIM)

        score = scores(kv_ref[:, ks], bias)
        top = jnp.max(score, axis=2, keepdims=True)
        if step_bias is not None:
            step_score = scores(step_ref[:, ks], step_bias)
            top = jnp.maximum(top, jnp.max(step_score, axis=2, keepdims=True))
        term = jnp.exp(score - top)
        total = jnp.sum(term, axis=2, keepdims=True)
        mixed = blend(term, kv_ref[:, vs])
        if step_bias is not None:
            step_term = jnp.exp(step_score - top)
            total = total + jnp.sum(step_term, axis=2, keepdims=True)
            mixed = mixed + blend(step_term, step_ref[:, vs])
        return mixed / total, top, total

    def record(g, top, total):
        lane = iota((top.shape[1], LANES), 1)
        stat = jnp.zeros(lane.shape, jnp.float32)
        for h in range(GROUP):
            stat = jnp.where(lane == g * GROUP + h, top[h], stat)
            stat = jnp.where(lane == half + g * GROUP + h, total[h], stat)
        return stat

    def swapped(stat):
        return jnp.concatenate([stat[:, half:], stat[:, :half]], axis=1)

    @pl.when(on_prefill)
    def _():
        row = iota((tokens, 1), 0)
        request = row >> 1
        turn = row & 1
        length = spread(request, lengths)

        def lanes_of(head):
            return slice(head * HEAD_DIM, (head + 1) * HEAD_DIM)

        def own(head):
            return q_ref[:, :, lanes_of(head)].reshape(tokens, HEAD_DIM)

        def passed(head):
            return partner_q[:, :, lanes_of(head)].reshape(tokens, HEAD_DIM)

        def serve(head, value):
            out_ref[:, lanes_of(head)] = value.astype(jnp.bfloat16)

        def keep(head, value):
            near_send[:, lanes_of(head)] = value

        q_to_partner.wait_recv()
        bias = bias_of(request, length)
        step_key = iota((tokens, tokens), 1)
        step_keep = ((step_key >> 1) == request) & ((step_key & 1) < turn + 1)
        step_bias = jnp.where(step_keep, 0.0, MASKED_SCORE)
        stat = jnp.zeros((tokens, LANES), jnp.float32)
        for g in range(KV_HEADS):
            heads = range(g * GROUP, (g + 1) * GROUP)
            query = jnp.concatenate([passed(head) for head in heads], axis=0)
            mixed, top, total = attend(g, query, bias, step_bias)
            for h, head in enumerate(heads):
                keep(head, mixed[h])
            stat = stat + record(g, top, total)
        near_stat_send[...] = stat
        o_to_partner.start()
        s_to_partner.start()
        bias = bias_of(request, length - 1 + turn)
        for g in range(KV_HEADS):
            heads = range(g * GROUP, (g + 1) * GROUP)
            query = jnp.concatenate([own(head) for head in heads], axis=0)
            mixed, _, _ = attend(g, query, bias)
            for h, head in enumerate(heads):
                serve(head, mixed[h])
        s_to_partner.wait_send()
        o_to_partner.wait_send()

    batch = min(8, n_seq)
    batch_rows = batch * per_peer

    def answer(c, g):
        steps = [n_seq - 1 - batch * c - i for i in range(batch)]
        peers = [peer_at(step) for step in steps]

        def unless_own(step, action):
            if isinstance(step, int):
                if step > 0:
                    action()
            else:
                pl.when(step > 0)(action)

        for step, peer in zip(steps, peers):
            unless_own(step, lambda peer=peer: slots_to(me, peer, g).wait_recv())

        def gathered(first):
            return jnp.concatenate(
                [arrived[peer, :, first : first + LANES].astype(jnp.float32) for peer in peers],
                axis=0,
            )

        rows = pl.ds(c * batch_rows, batch_rows)
        if g == 0:
            group = gathered(0).astype(jnp.int32)[:, 0:1]
            slot_bias[rows, :] = bias_of(group, spread(group, cuts))
        query = jnp.concatenate(
            [
                gathered(LANES + head * HEAD_DIM).astype(jnp.bfloat16)
                for head in range(g * GROUP, (g + 1) * GROUP)
            ],
            axis=0,
        )
        mixed, top, total = attend(g, query, slot_bias[rows, :])
        for h in range(GROUP):
            head = g * GROUP + h
            for i, peer in enumerate(peers):
                ret_send[peer, :, head * HEAD_DIM : (head + 1) * HEAD_DIM] = mixed[
                    h, i * per_peer : (i + 1) * per_peer
                ].astype(jnp.bfloat16)
        stat = record(g, top, total)
        for i, peer in enumerate(peers):
            part = stat[i * per_peer : (i + 1) * per_peer]
            ret_stat_send[peer] = part if g == 0 else ret_stat_send[peer] + part

        def reply(peer):
            if g == KV_HEADS - 1:
                stat_to(peer, me).start()
            out_to(peer, me, g).start()

        for step, peer in zip(steps, peers):
            unless_own(step, lambda peer=peer: reply(peer))

    @pl.when(on_decode)
    def _():
        for g in range(KV_HEADS):
            if n_seq == batch:
                answer(0, g)
            else:

                def one(c, carry):
                    answer(c, g)
                    return carry

                lax.fori_loop(0, n_seq // batch, one, 0)

    @pl.when(on_decode)
    def _():
        ret[pl.ds(me, 1)] = ret_send[pl.ds(me, 1)]
        ret_stat[pl.ds(me, 1)] = ret_stat_send[pl.ds(me, 1)]
        tok = iota((tokens, 1), 0)
        target = 2 * spread(tok >> 1, places) + (tok & 1)
        unpick = jnp.where(iota((tokens, slot_rows), 1) == target, 1.0, 0.0)
        o_to_partner.wait_recv()
        s_to_partner.wait_recv()
        pick_back = unpick.astype(jnp.bfloat16)
        for g in range(KV_HEADS):
            for step in range(n_seq - 1, 0, -1):
                out_to(me, peer_at(step), g).wait_recv()
            for head in range(g * GROUP, (g + 1) * GROUP):
                part = slice(head * HEAD_DIM, (head + 1) * HEAD_DIM)
                came = jnp.concatenate(
                    [ret[s, :, part].astype(jnp.float32) for s in range(n_seq)], axis=0
                ).astype(jnp.bfloat16)
                far_out[:, part] = jnp.dot(pick_back, came, preferred_element_type=jnp.float32)
        for step in range(n_seq - 1, 0, -1):
            stat_to(me, peer_at(step)).wait_recv()
        back = jnp.concatenate([ret_stat[s] for s in range(n_seq)], axis=0)
        far_top = jnp.dot(
            unpick, back, preferred_element_type=jnp.float32, precision=lax.Precision.HIGHEST
        )
        far_sum = swapped(far_top)
        near_top = partner_stat[...]
        near_sum = swapped(near_top)
        top = jnp.maximum(far_top, near_top)
        far_weight = far_sum * jnp.exp(far_top - top)
        near_weight = near_sum * jnp.exp(near_top - top)
        total = jnp.where(near_weight + far_weight == 0.0, 1.0, near_weight + far_weight)
        far_share = far_weight / total
        near_share = near_weight / total
        for head in range(heads_all):
            part = slice(head * HEAD_DIM, (head + 1) * HEAD_DIM)
            out_ref[:, part] = (
                far_out[:, part] * far_share[:, head : head + 1]
                + partner_o[:, part] * near_share[:, head : head + 1]
            ).astype(jnp.bfloat16)
        q_to_partner.wait_send()
        for step in range(1, n_seq):
            peer = peer_at(step)
            for g in range(KV_HEADS):
                slots_to(peer, me, g).wait_send()
                out_to(peer, me, g).wait_send()
            stat_to(peer, me).wait_send()


def local(
    kv_store, queries, step_kv, suffix_pages, suffix_len, owner, parent_id, parent_pages, parent_len
):
    n_seq = lax.axis_size("seq")
    page_store = kv_store[0]
    requests, turns, q_width = queries.shape[1:]
    tokens = requests * turns
    cap = max(4, 2 * requests // n_seq)
    per_peer = 2 * cap
    bf16, f32 = jnp.bfloat16, jnp.float32
    vmem = pl.BlockSpec(memory_space=pltpu.VMEM)
    hbm = pl.BlockSpec(memory_space=pl.ANY)
    dma = pltpu.SemaphoreType.DMA
    served = pl.pallas_call(
        functools.partial(kernel, n_seq, cap),
        out_shape=jax.ShapeDtypeStruct((tokens, q_width), bf16),
        in_specs=[hbm] * 9,
        out_specs=vmem,
        scratch_shapes=[
            pltpu.SMEM((requests,), jnp.int32),
            pltpu.SMEM((requests,), jnp.int32),
            pltpu.SMEM((requests,), jnp.int32),
            pltpu.SMEM(suffix_pages.shape[::-1], jnp.int32),
            pltpu.SMEM(parent_pages.shape, jnp.int32),
            pltpu.SMEM(parent_len.shape, jnp.int32),
            pltpu.VMEM((requests, turns, q_width), bf16),
            pltpu.VMEM(page_store.shape, bf16),
            pltpu.VMEM(step_kv.shape, bf16),
            pltpu.VMEM((tokens, step_kv.shape[2]), bf16),
            pltpu.VMEM((n_seq, per_peer, q_width + LANES), bf16),
            pltpu.VMEM((n_seq, per_peer, q_width + LANES), bf16),
            pltpu.VMEM((8, page_store.shape[0]), jnp.int32),
            pltpu.VMEM((n_seq * per_peer, page_store.shape[0]), f32),
            pltpu.VMEM((tokens, q_width), f32),
            pltpu.VMEM((tokens, q_width), f32),
            pltpu.VMEM((tokens, LANES), f32),
            pltpu.VMEM((n_seq, per_peer, q_width), bf16),
            pltpu.VMEM((n_seq, per_peer, LANES), f32),
            pltpu.VMEM((n_seq, per_peer, q_width), bf16),
            pltpu.VMEM((n_seq, per_peer, LANES), f32),
            pltpu.VMEM((requests, turns, q_width), bf16),
            pltpu.VMEM((tokens, q_width), f32),
            pltpu.VMEM((tokens, LANES), f32),
            dma((9,)),
            dma((n_seq, KV_HEADS)),
            dma((n_seq, KV_HEADS)),
            dma((n_seq, KV_HEADS)),
            dma((n_seq, KV_HEADS)),
            dma((n_seq,)),
            dma((n_seq,)),
            dma((3,)),
            dma((3,)),
        ],
        compiler_params=pltpu.CompilerParams(
            collective_id=0, has_side_effects=True, vmem_limit_bytes=60 * 1024 * 1024
        ),
    )(
        owner.reshape(-1),
        parent_id,
        suffix_len,
        suffix_pages.T,
        parent_pages,
        parent_len,
        queries[0],
        page_store,
        step_kv,
    )
    return served.reshape(1, requests, turns, q_width)


def solution(mesh):
    in_specs = (
        P("role", ("groups", "seq"), None),
        P("role", ("groups", "seq"), None, None),
        P(("groups", "seq"), None, None),
        P(("groups", "seq"), None),
        P(("groups", "seq")),
        P(("groups", "seq"), None),
        P(("groups", "seq")),
        P(("groups", "seq"), None),
        P(("groups", "seq")),
    )
    out_specs = P("role", ("groups", "seq"), None, None)
    return jax.shard_map(local, mesh=mesh, in_specs=in_specs, out_specs=out_specs, check_vma=False)
```

```python
import functools

import jax
import jax.numpy as jnp
from jax import lax
from jax.experimental import pallas as pl
from jax.experimental.pallas import tpu as pltpu
from jax.sharding import PartitionSpec as P

HEAD_DIM = 128
KV_HEADS = 4
GROUP = 8
PAGE = 16
LANES = 128

MASKED_SCORE = -1e30
MESH = pl.DeviceIdType.MESH


def iota(shape, dim):
    return lax.broadcasted_iota(jnp.int32, shape, dim)


def spread(index, scalars):
    out = jnp.zeros(index.shape, jnp.int32)
    for i, scalar in enumerate(scalars):
        out = jnp.where(index == i, scalar, out)
    return out


def kernel(
    n_seq,
    cap,
    owner_hbm,
    parent_id_hbm,
    suffix_len_hbm,
    suffix_pages_hbm,
    parent_pages_hbm,
    parent_len_hbm,
    q_hbm,
    kv_hbm,
    step_hbm,
    out_ref,
    owner,
    parent_id,
    suffix_len,
    suffix_pages,
    parent_pages,
    parent_len,
    q_ref,
    kv_ref,
    step_in,
    step_ref,
    slots,
    arrived,
    key_meta,
    slot_bias,
    far_out,
    near_send,
    near_stat_send,
    ret_send,
    ret_stat_send,
    ret,
    ret_stat,
    partner_q,
    partner_o,
    partner_stat,
    load_sem,
    send_sem,
    recv_sem,
    osend_sem,
    orecv_sem,
    ssend_sem,
    srecv_sem,
    psend_sem,
    precv_sem,
):
    role = lax.axis_index("role")
    me = lax.axis_index("seq")
    requests, turns, q_width = q_ref.shape
    tokens = requests * turns
    per_peer = 2 * cap
    slot_rows = n_seq * per_peer
    key_count = kv_ref.shape[0]
    key_width = KV_HEADS * HEAD_DIM
    scale = HEAD_DIM ** (-0.5)
    partner = {"role": 1 - role}
    on_decode = role == 1
    on_prefill = role == 0
    heads_all = KV_HEADS * GROUP
    group_width = GROUP * HEAD_DIM
    half = LANES // 2

    bits = [(me // 2**b) % 2 for b in range(n_seq.bit_length() - 1)]

    def peer_at(step):
        if n_seq & (n_seq - 1):
            return lax.rem(me + step, n_seq)
        peer = me
        for b, mine in enumerate(bits):
            if isinstance(step, int):
                if (step >> b) & 1:
                    peer = peer + 2**b * (1 - 2 * mine)
            else:
                peer = peer + 2**b * (1 - 2 * mine) * ((step // 2**b) % 2)
        return peer

    barrier = pltpu.get_barrier_semaphore()
    @pl.when(on_decode)
    def _():
        for step in range(n_seq - 1, 0, -1):
            pl.semaphore_signal(
                barrier, inc=1, device_id={"seq": peer_at(step)}, device_id_type=MESH
            )

    pl.semaphore_signal(barrier, inc=1, device_id=partner, device_id_type=MESH)

    load_q = pltpu.make_async_copy(q_hbm, q_ref, load_sem.at[0])
    load_step = pltpu.make_async_copy(step_hbm, step_in, load_sem.at[1])
    load_kv = pltpu.make_async_copy(kv_hbm, kv_ref, load_sem.at[2])
    tables = [
        pltpu.make_async_copy(src, dst, load_sem.at[3 + i])
        for i, (src, dst) in enumerate(
            (
                (owner_hbm, owner),
                (parent_id_hbm, parent_id),
                (suffix_len_hbm, suffix_len),
                (suffix_pages_hbm, suffix_pages),
                (parent_pages_hbm, parent_pages),
                (parent_len_hbm, parent_len),
            )
        )
    ]
    load_q.start()
    for table in tables:
        table.start()
    load_step.start()
    load_kv.start()

    def remote(src, dst, ssem, rsem, device):
        return pltpu.make_async_remote_copy(
            src_ref=src,
            dst_ref=dst,
            send_sem=ssem,
            recv_sem=rsem,
            device_id=device,
            device_id_type=MESH,
        )

    q_to_partner = remote(q_ref, partner_q, psend_sem.at[0], precv_sem.at[0], partner)
    o_to_partner = remote(near_send, partner_o, psend_sem.at[1], precv_sem.at[1], partner)
    s_to_partner = remote(near_stat_send, partner_stat, psend_sem.at[2], precv_sem.at[2], partner)

    def q_lanes(g):
        first = 0 if g == 0 else LANES + g * group_width
        return slice(first, LANES + (g + 1) * group_width)

    def slots_to(peer, mine, g):
        return remote(
            slots.at[peer, :, q_lanes(g)],
            arrived.at[mine, :, q_lanes(g)],
            send_sem.at[peer, g],
            recv_sem.at[mine, g],
            {"seq": peer},
        )

    def out_to(peer, mine, g):
        lanes = slice(g * group_width, (g + 1) * group_width)
        return remote(
            ret_send.at[peer, :, lanes],
            ret.at[mine, :, lanes],
            osend_sem.at[peer, g],
            orecv_sem.at[mine, g],
            {"seq": peer},
        )

    def stat_to(peer, mine):
        return remote(
            ret_stat_send.at[peer],
            ret_stat.at[mine],
            ssend_sem.at[peer],
            srecv_sem.at[mine],
            {"seq": peer},
        )

    for table in tables:
        table.wait()
    owners = [owner[r] for r in range(requests)]
    places = []
    for r in range(requests):
        rank = jnp.int32(0)
        for e in range(r):
            rank = rank + jnp.where(owners[e] == owners[r], 1, 0)
        places.append(owners[r] * cap + rank)
    lengths = [suffix_len[r] for r in range(requests)]
    parents = [parent_id[r] for r in range(requests)]

    load_q.wait()

    @pl.when(on_decode)
    def _():
        col = iota((1, tokens), 1)
        target = 2 * spread(col >> 1, places) + (col & 1)
        pick = jnp.where(iota((slot_rows, tokens), 0) == target, 1.0, 0.0).astype(jnp.bfloat16)
        tok = iota((tokens, LANES), 0) >> 1
        pid = spread(tok, parents).astype(jnp.float32).astype(jnp.bfloat16)
        pid_slots = jnp.dot(pick, pid, preferred_element_type=jnp.float32)
        for d in range(n_seq):
            slots[d, :, :LANES] = pid_slots[d * per_peer : (d + 1) * per_peer].astype(
                jnp.bfloat16
            )
        block = 4 * LANES
        for c in range(q_width // block):
            lanes = slice(c * block, (c + 1) * block)
            part = jnp.dot(
                pick, q_ref[:, :, lanes].reshape(tokens, block), preferred_element_type=jnp.float32
            )
            for d in range(n_seq):
                slots[d, :, LANES + c * block : LANES + (c + 1) * block] = part[d * per_peer : (d + 1) * per_peer].astype(jnp.bfloat16)
        pl.semaphore_wait(barrier, n_seq)
        q_to_partner.start()
        for g in range(KV_HEADS):
            for step in range(n_seq - 1, 0, -1):
                slots_to(peer_at(step), me, g).start()
        arrived[pl.ds(me, 1)] = slots[pl.ds(me, 1)]

    @pl.when(on_prefill)
    def _():
        pl.semaphore_wait(barrier, 1)

    lane_page = iota((1, key_count), 1) // PAGE
    group_row = jnp.zeros((1, key_count), jnp.int32)
    base_row = jnp.zeros((1, key_count), jnp.int32)
    suf_pages = suffix_pages.shape[0]
    par_pages = parent_pages.shape[1]
    for j in range(key_count // PAGE):
        page = jnp.where(
            on_prefill,
            suffix_pages[j % suf_pages, j // suf_pages],
            parent_pages[j // par_pages, j % par_pages],
        )
        here = lane_page == page
        group_row = jnp.where(here, jnp.where(on_prefill, j // suf_pages, j // par_pages), group_row)
        base_row = jnp.where(
            here, jnp.where(on_prefill, j % suf_pages, j % par_pages) * PAGE, base_row
        )
    pos_row = base_row + (iota((1, key_count), 1) & (PAGE - 1))
    key_meta[0:1, :] = group_row
    key_meta[1:2, :] = pos_row
    load_step.wait()
    for c in range(step_ref.shape[1] // (4 * LANES)):
        lanes = slice(c * 4 * LANES, (c + 1) * 4 * LANES)
        step_ref[:, lanes] = step_in[:, :, lanes].reshape(tokens, 4 * LANES)
    cuts = [parent_len[a] for a in range(parent_len.shape[0])]
    load_kv.wait()

    def bias_of(group, limit):
        keep = (key_meta[0:1, :] == group) & (key_meta[1:2, :] < limit)
        return jnp.where(keep, 0.0, MASKED_SCORE)

    def attend(g, query, bias, step_bias=None):
        rows = bias.shape[0]
        ks = slice(g * HEAD_DIM, (g + 1) * HEAD_DIM)
        vs = slice(key_width + g * HEAD_DIM, key_width + (g + 1) * HEAD_DIM)
        contract = (((1,), (1,)), ((), ()))

        def scores(keys, add):
            found = lax.dot_general(query, keys, contract, preferred_element_type=jnp.float32)
            return found.reshape(GROUP, rows, keys.shape[0]) * scale + add[None]

        def blend(term, values):
            term = term.reshape(GROUP * rows, values.shape[0]).astype(jnp.bfloat16)
            mixed = jnp.dot(term, values, preferred_element_type=jnp.float32)
            return mixed.reshape(GROUP, rows, HEAD_DIM)

        score = scores(kv_ref[:, ks], bias)
        top = jnp.max(score, axis=2, keepdims=True)
        if step_bias is not None:
            step_score = scores(step_ref[:, ks], step_bias)
            top = jnp.maximum(top, jnp.max(step_score, axis=2, keepdims=True))
        term = jnp.exp(score - top)
        total = jnp.sum(term, axis=2, keepdims=True)
        mixed = blend(term, kv_ref[:, vs])
        if step_bias is not None:
            step_term = jnp.exp(step_score - top)
            total = total + jnp.sum(step_term, axis=2, keepdims=True)
            mixed = mixed + blend(step_term, step_ref[:, vs])
        return mixed / total, top, total

    def record(g, top, total):
        lane = iota((top.shape[1], LANES), 1)
        stat = jnp.zeros(lane.shape, jnp.float32)
        for h in range(GROUP):
            stat = jnp.where(lane == g * GROUP + h, top[h], stat)
            stat = jnp.where(lane == half + g * GROUP + h, total[h], stat)
        return stat

    def swapped(stat):
        return jnp.concatenate([stat[:, half:], stat[:, :half]], axis=1)

    @pl.when(on_prefill)
    def _():
        row = iota((tokens, 1), 0)
        request = row >> 1
        turn = row & 1
        length = spread(request, lengths)

        def lanes_of(head):
            return slice(head * HEAD_DIM, (head + 1) * HEAD_DIM)

        def own(head):
            return q_ref[:, :, lanes_of(head)].reshape(tokens, HEAD_DIM)

        def passed(head):
            return partner_q[:, :, lanes_of(head)].reshape(tokens, HEAD_DIM)

        def serve(head, value):
            out_ref[:, lanes_of(head)] = value.astype(jnp.bfloat16)

        def keep(head, value):
            near_send[:, lanes_of(head)] = value

        q_to_partner.wait_recv()
        bias = bias_of(request, length)
        step_key = iota((tokens, tokens), 1)
        step_keep = ((step_key >> 1) == request) & ((step_key & 1) < turn + 1)
        step_bias = jnp.where(step_keep, 0.0, MASKED_SCORE)
        stat = jnp.zeros((tokens, LANES), jnp.float32)
        for g in range(KV_HEADS):
            heads = range(g * GROUP, (g + 1) * GROUP)
            query = jnp.concatenate([passed(head) for head in heads], axis=0)
            mixed, top, total = attend(g, query, bias, step_bias)
            for h, head in enumerate(heads):
                keep(head, mixed[h])
            stat = stat + record(g, top, total)
        near_stat_send[...] = stat
        o_to_partner.start()
        s_to_partner.start()
        bias = bias_of(request, length - 1 + turn)
        for g in range(KV_HEADS):
            heads = range(g * GROUP, (g + 1) * GROUP)
            query = jnp.concatenate([own(head) for head in heads], axis=0)
            mixed, _, _ = attend(g, query, bias)
            for h, head in enumerate(heads):
                serve(head, mixed[h])
        s_to_partner.wait_send()
        o_to_partner.wait_send()

    batch = min(8, n_seq)
    batch_rows = batch * per_peer

    def answer(c, g):
        steps = [n_seq - 1 - batch * c - i for i in range(batch)]
        peers = [peer_at(step) for step in steps]

        def unless_own(step, action):
            if isinstance(step, int):
                if step > 0:
                    action()
            else:
                pl.when(step > 0)(action)

        for step, peer in zip(steps, peers):
            unless_own(step, lambda peer=peer: slots_to(me, peer, g).wait_recv())

        def gathered(first):
            return jnp.concatenate(
                [arrived[peer, :, first : first + LANES].astype(jnp.float32) for peer in peers],
                axis=0,
            )

        rows = pl.ds(c * batch_rows, batch_rows)
        if g == 0:
            group = gathered(0).astype(jnp.int32)[:, 0:1]
            slot_bias[rows, :] = bias_of(group, spread(group, cuts))
        query = jnp.concatenate(
            [
                gathered(LANES + head * HEAD_DIM).astype(jnp.bfloat16)
                for head in range(g * GROUP, (g + 1) * GROUP)
            ],
            axis=0,
        )
        mixed, top, total = attend(g, query, slot_bias[rows, :])
        for h in range(GROUP):
            head = g * GROUP + h
            for i, peer in enumerate(peers):
                ret_send[peer, :, head * HEAD_DIM : (head + 1) * HEAD_DIM] = mixed[
                    h, i * per_peer : (i + 1) * per_peer
                ].astype(jnp.bfloat16)
        stat = record(g, top, total)
        for i, peer in enumerate(peers):
            part = stat[i * per_peer : (i + 1) * per_peer]
            ret_stat_send[peer] = part if g == 0 else ret_stat_send[peer] + part

        def reply(peer):
            if g == KV_HEADS - 1:
                stat_to(peer, me).start()
            out_to(peer, me, g).start()

        for step, peer in zip(steps, peers):
            unless_own(step, lambda peer=peer: reply(peer))

    @pl.when(on_decode)
    def _():
        for g in range(KV_HEADS):
            if n_seq == batch:
                answer(0, g)
            else:

                def one(c, carry):
                    answer(c, g)
                    return carry

                lax.fori_loop(0, n_seq // batch, one, 0)

    @pl.when(on_decode)
    def _():
        ret[pl.ds(me, 1)] = ret_send[pl.ds(me, 1)]
        ret_stat[pl.ds(me, 1)] = ret_stat_send[pl.ds(me, 1)]
        tok = iota((tokens, 1), 0)
        target = 2 * spread(tok >> 1, places) + (tok & 1)
        unpick = jnp.where(iota((tokens, slot_rows), 1) == target, 1.0, 0.0)
        o_to_partner.wait_recv()
        s_to_partner.wait_recv()
        pick_back = unpick.astype(jnp.bfloat16)
        for g in range(KV_HEADS):
            for step in range(n_seq - 1, 0, -1):
                out_to(me, peer_at(step), g).wait_recv()
            for head in range(g * GROUP, (g + 1) * GROUP):
                part = slice(head * HEAD_DIM, (head + 1) * HEAD_DIM)
                came = jnp.concatenate(
                    [ret[s, :, part].astype(jnp.float32) for s in range(n_seq)], axis=0
                ).astype(jnp.bfloat16)
                far_out[:, part] = jnp.dot(pick_back, came, preferred_element_type=jnp.float32)
        for step in range(n_seq - 1, 0, -1):
            stat_to(me, peer_at(step)).wait_recv()
        back = jnp.concatenate([ret_stat[s] for s in range(n_seq)], axis=0)
        far_top = jnp.dot(
            unpick, back, preferred_element_type=jnp.float32, precision=lax.Precision.HIGHEST
        )
        far_sum = swapped(far_top)
        near_top = partner_stat[...]
        near_sum = swapped(near_top)
        top = jnp.maximum(far_top, near_top)
        far_weight = far_sum * jnp.exp(far_top - top)
        near_weight = near_sum * jnp.exp(near_top - top)
        total = jnp.where(near_weight + far_weight == 0.0, 1.0, near_weight + far_weight)
        far_share = far_weight / total
        for head in range(heads_all):
            part = slice(head * HEAD_DIM, (head + 1) * HEAD_DIM)
            near = partner_o[:, part]
            out_ref[:, part] = (
                near + (far_out[:, part] - near) * far_share[:, head : head + 1]
            ).astype(jnp.bfloat16)
        q_to_partner.wait_send()
        for step in range(1, n_seq):
            peer = peer_at(step)
            for g in range(KV_HEADS):
                slots_to(peer, me, g).wait_send()
                out_to(peer, me, g).wait_send()
            stat_to(peer, me).wait_send()


def local(
    kv_store, queries, step_kv, suffix_pages, suffix_len, owner, parent_id, parent_pages, parent_len
):
    n_seq = lax.axis_size("seq")
    page_store = kv_store[0]
    requests, turns, q_width = queries.shape[1:]
    tokens = requests * turns
    cap = max(4, 2 * requests // n_seq)
    per_peer = 2 * cap
    bf16, f32 = jnp.bfloat16, jnp.float32
    vmem = pl.BlockSpec(memory_space=pltpu.VMEM)
    hbm = pl.BlockSpec(memory_space=pl.ANY)
    dma = pltpu.SemaphoreType.DMA
    served = pl.pallas_call(
        functools.partial(kernel, n_seq, cap),
        out_shape=pltpu.VMEM((tokens, q_width), bf16),
        in_specs=[hbm] * 9,
        out_specs=vmem,
        scratch_shapes=[
            pltpu.SMEM((requests,), jnp.int32),
            pltpu.SMEM((requests,), jnp.int32),
            pltpu.SMEM((requests,), jnp.int32),
            pltpu.SMEM(suffix_pages.shape[::-1], jnp.int32),
            pltpu.SMEM(parent_pages.shape, jnp.int32),
            pltpu.SMEM(parent_len.shape, jnp.int32),
            pltpu.VMEM((requests, turns, q_width), bf16),
            pltpu.VMEM(page_store.shape, bf16),
            pltpu.VMEM(step_kv.shape, bf16),
            pltpu.VMEM((tokens, step_kv.shape[2]), bf16),
            pltpu.VMEM((n_seq, per_peer, q_width + LANES), bf16),
            pltpu.VMEM((n_seq, per_peer, q_width + LANES), bf16),
            pltpu.VMEM((8, page_store.shape[0]), jnp.int32),
            pltpu.VMEM((n_seq * per_peer, page_store.shape[0]), f32),
            pltpu.VMEM((tokens, q_width), f32),
            pltpu.VMEM((tokens, q_width), f32),
            pltpu.VMEM((tokens, LANES), f32),
            pltpu.VMEM((n_seq, per_peer, q_width), bf16),
            pltpu.VMEM((n_seq, per_peer, LANES), f32),
            pltpu.VMEM((n_seq, per_peer, q_width), bf16),
            pltpu.VMEM((n_seq, per_peer, LANES), f32),
            pltpu.VMEM((requests, turns, q_width), bf16),
            pltpu.VMEM((tokens, q_width), f32),
            pltpu.VMEM((tokens, LANES), f32),
            dma((9,)),
            dma((n_seq, KV_HEADS)),
            dma((n_seq, KV_HEADS)),
            dma((n_seq, KV_HEADS)),
            dma((n_seq, KV_HEADS)),
            dma((n_seq,)),
            dma((n_seq,)),
            dma((3,)),
            dma((3,)),
        ],
        compiler_params=pltpu.CompilerParams(
            collective_id=0, has_side_effects=True, vmem_limit_bytes=60 * 1024 * 1024
        ),
    )(
        owner.reshape(-1),
        parent_id,
        suffix_len,
        suffix_pages.T,
        parent_pages,
        parent_len,
        queries[0],
        page_store,
        step_kv,
    )
    return served.reshape(1, requests, turns, q_width)


def solution(mesh):
    in_specs = (
        P("role", ("groups", "seq"), None),
        P("role", ("groups", "seq"), None, None),
        P(("groups", "seq"), None, None),
        P(("groups", "seq"), None),
        P(("groups", "seq")),
        P(("groups", "seq"), None),
        P(("groups", "seq")),
        P(("groups", "seq"), None),
        P(("groups", "seq")),
    )
    out_specs = P("role", ("groups", "seq"), None, None)
    return jax.shard_map(local, mesh=mesh, in_specs=in_specs, out_specs=out_specs, check_vma=False)
```
